32 devices in a mesh: scene: 2 (over y), az: 8 (over z, x), rg: 2 (over core).
Axes of the slice: x: 2, y: 2, z: 4, core: 2. Of those that a mesh axis runs over, the one named last changes fastest.
Arguments:
- raw_re: float32 [64, 32768], P('rg', ('scene', 'az')), parts along dimension 1, may hold values from -6 to 6
- raw_im: float32 [64, 32768], P('rg', ('scene', 'az')), parts along dimension 1, may hold values from -6 to 6
- ref_blocks: float32 [16, 64, 64], P(('scene', 'az'), None, 'rg'), parts along dimension 0, may hold values from -3.140625 to 3.140625
- owners: int32 [4], P('scene'), parts along dimension 0, may hold values from 0 to 7, as said below
- offsets: int32 [4], P('rg'), may hold values from -8 to 8
- taps: float32 [64, 8], P('rg'), may hold values from -3 to 3
Outputs:
- image_re: float32 [64, 32768], P('rg', ('scene', 'az')), parts along dimension 1
- image_im: float32 [64, 32768], P('rg', ('scene', 'az')), parts along dimension 1
The draws below stay inside these ranges and needn't reach their ends.
There are 2 independent parts, one for each index of `scene`. The reference program is written for one: setup_inputs(seed, part) draws one part's arguments, and reference() takes and returns one part's arrays. A program takes and returns all parts, laid end to end along the dimension named above; an argument that names none is the same for every part. Nothing has to cross between parts.
Inputs may be any that keep to these rules, and one draw needn't show every extreme that they name: The two sub-apertures have different owners.
All inputs are finite; a program needn't handle non-finite values.
Results may differ from the reference program's by a relative error of at most 0.00014.
Values sent between devices are 32-bit elements; how exact they have to be, the bound alone decides.
A program may use at most 64 MiB of HBM per device.

```python
import jax
import jax.numpy as jnp
from jax import lax

TAPS = 8
REACH = 8
BLOCK = 16
REF_ROWS = 64
NA = 16384
NR = 64
NBLK = 4
N_AZ = 8


def draw_owners(key, part):
    other_key = jax.random.fold_in(key, 11)
    slot_key = jax.random.fold_in(key, 23)
    other = jax.random.randint(other_key, (), 0, N_AZ - 1, dtype=jnp.int32)
    last = jnp.full((), N_AZ - 1, dtype=jnp.int32)
    which = jax.random.randint(slot_key, (), 0, 2, dtype=jnp.int32)
    first = jnp.where(which == 0, last, other)
    second = jnp.where(which == 0, other, last)
    return jnp.stack([first, second]).astype(jnp.int32)


def set_ends(array, key, least, largest):
    extent = array.shape
    index_at = [jax.random.randint(jax.random.fold_in(key, axis), (), 0, extent[axis]) for axis in range(len(extent))]
    array = array.at[tuple(index_at)].set(least)
    longest = extent.index(max(extent))
    index_at[longest] = (index_at[longest] + 1) % extent[longest]
    return array.at[tuple(index_at)].set(largest)


def levels(key, dims, split, least, largest):
    level, own = 1.0, jax.random.fold_in(key, 6)
    for axis_at, blocks in split:
        draws = jnp.exp(jax.random.uniform(jax.random.fold_in(own, axis_at), (blocks,), jnp.float32, least / len(split), largest / len(split)))
        level = level * jnp.repeat(draws, dims[axis_at] // blocks).reshape([-1 if axis == axis_at else 1 for axis in range(len(dims))])
    return level


def bell_draw(rng, extent, deviation, most, split=(), kind=jnp.bfloat16):
    array = jax.random.normal(rng, extent, jnp.float32) * deviation
    if len(split) > 0:
        array = levels(rng, extent, split, -0.22, 0.18) * array
    return jnp.clip(array, min=-most, max=most).astype(kind)


def setup_inputs(seed: int = 0, part: int = 0) -> dict:
    arg_keys = jax.random.split(jax.random.key(seed), 7)
    part_keys = jax.random.split(jax.random.fold_in(arg_keys[6], part), 7)
    raw_re = bell_draw(part_keys[0], (NR, NA), 1.0, 6.0, ((0, 2), (1, 8)), jnp.float32)
    raw_im = bell_draw(part_keys[1], (NR, NA), 1.0, 6.0, ((0, 2), (1, 8)), jnp.float32)
    ref_blocks = jnp.clip(jax.random.uniform(part_keys[2], (N_AZ, REF_ROWS, NR), jnp.float32, -3.140625, 3.140625), -3.140625, 3.140625)
    owners = draw_owners(jax.random.fold_in(jax.random.fold_in(arg_keys[6], part), 71), part)
    offsets = set_ends(jax.random.randint(arg_keys[4], (NBLK,), 0 - REACH, REACH + 1), jax.random.fold_in(arg_keys[4], 1), 0 - REACH, REACH).astype(jnp.int32)
    taps = bell_draw(arg_keys[5], (NR, TAPS), 0.5, 3.0, ((0, 2),), jnp.float32)
    return dict(raw_re=raw_re, raw_im=raw_im, ref_blocks=ref_blocks, owners=owners, offsets=offsets, taps=taps)


PHASE_GAIN = 50.0

def reference(raw_re, raw_im, ref_blocks, owners, offsets, taps):
    rg_total = raw_re.shape[0]
    az_total = raw_re.shape[1]
    spectrum = jnp.fft.fft(lax.complex(raw_re, raw_im), axis=1)
    frequency = jnp.arange(az_total, dtype=jnp.int32)
    signed = (frequency + az_total // 2) % az_total - az_total // 2
    az_freq = signed.astype(jnp.float32) / az_total
    rg_index = jnp.arange(rg_total, dtype=jnp.int32)
    rg_freq = (rg_index.astype(jnp.float32) + 0.5) / (2 * rg_total) - 0.25
    model_phase = PHASE_GAIN * jnp.sqrt((1.0 + rg_freq)[:, None] ** 2 - az_freq[None, :] ** 2)
    chosen = ref_blocks[owners]
    coarse = frequency * REF_ROWS // az_total
    picked = jnp.where((signed >= 0)[None, :], chosen[1][coarse].T, chosen[0][coarse].T)
    phase_all = model_phase + picked
    matched = spectrum * lax.complex(jnp.cos(phase_all), jnp.sin(phase_all))
    rim_width = REACH + TAPS // 2
    padded = jnp.pad(matched, ((rim_width, rim_width), (0, 0)))
    offset_cols = jnp.repeat(offsets, BLOCK)
    stolt = jnp.zeros_like(matched)
    for tap_num in range(TAPS):
        source = rg_index + rim_width + offset_cols + tap_num - TAPS // 2
        stolt = stolt + taps[:, tap_num][:, None] * padded[source, :]
    image = jnp.fft.ifft(stolt, axis=1)
    return (image.real, image.imag)
```

```python
import functools
import math

import jax
import jax.numpy as jnp
import ml_dtypes
import numpy as np
from jax import lax
from jax.experimental import pallas as pl
from jax.experimental.pallas import tpu as pltpu
from jax.sharding import PartitionSpec as P

SPLIT = 4
TAPS = 8
REACH = 8
BLOCK = 16


PRECISE = lax.Precision.HIGHEST
PHASE_GAIN = 50.0


def partner_2(value, axis, stride):
    return lax.ppermute(value, axis, [(i, i ^ 1 << stride) for i in range(lax.axis_size(axis))])


def from_root(block, axis, source):
    block = jnp.where(lax.axis_index(axis) == source, block, jnp.zeros_like(block))
    return lax.psum(block, axis)


def padded_2(value, sides, width):
    for axis, dim in sides:
        size, length = (lax.axis_size(axis), value.shape[dim])
        up = [(i, (i + 1) % size) for i in range(size - 1)]
        down = [(j, i) for i, j in up]
        last = lax.slice_in_dim(value, length - width, length, axis=dim)
        initial = lax.slice_in_dim(value, 0, width, axis=dim)
        before = lax.ppermute(last, axis, up)
        after = lax.ppermute(initial, axis, down)
        value = jnp.concatenate([before, value, after], axis=dim)
    return value


def angles(numerator, denominator, sign_value):
    return sign_value * 2.0 * math.pi * numerator.astype(jnp.float32) / denominator


def rotate(signal, cosine, sine_part):
    real_part = signal[0] * cosine - signal[1] * sine_part
    imag_part = signal[0] * sine_part + signal[1] * cosine
    return jnp.stack([real_part, imag_part])


def dft_table(length_n, sign_value):
    counter = jnp.arange(length_n, dtype=jnp.int32)
    turn_count = counter[:, None] * counter[None, :] % length_n
    angle_set = angles(turn_count, length_n, sign_value)
    return (jnp.cos(angle_set), jnp.sin(angle_set))


def complex_apply(einsum_form, cosine, sine_part, signal):
    real_part = jnp.einsum(einsum_form, cosine, signal[0], precision=PRECISE) - jnp.einsum(
        einsum_form, sine_part, signal[1], precision=PRECISE
    )
    imag_part = jnp.einsum(einsum_form, cosine, signal[1], precision=PRECISE) + jnp.einsum(
        einsum_form, sine_part, signal[0], precision=PRECISE
    )
    return jnp.stack([real_part, imag_part])


def local_dft(signal, sign_value):
    rg_cols = signal.shape[1]
    az_rows = signal.shape[2]
    inner_len = az_rows // SPLIT
    shaped = signal.reshape(2, rg_cols, SPLIT, inner_len)
    first_cos, first_sin = dft_table(SPLIT, sign_value)
    first_pass = complex_apply("aj,cjk->cak", first_cos, first_sin, shaped)
    outer_idx = jnp.arange(SPLIT, dtype=jnp.int32)
    inner_idx = jnp.arange(inner_len, dtype=jnp.int32)
    twist = angles(outer_idx[:, None] * inner_idx[None, :] % az_rows, az_rows, sign_value)
    first_pass = rotate(first_pass, jnp.cos(twist)[None, :, :], jnp.sin(twist)[None, :, :])
    second_cos, second_sin = dft_table(inner_len, sign_value)
    second_pass = complex_apply("bk,cak->cba", second_cos, second_sin, first_pass)
    return second_pass.reshape(2, rg_cols, az_rows)


def butterfly_down(signal, az_place, bit_count):
    for bit_num in reversed(range(bit_count)):
        half_span = 1 << bit_num
        partner = partner_2(signal, "az", bit_num)
        is_upper = az_place >> bit_num & 1 == 1
        angle_set = angles(az_place % half_span, 2 * half_span, -1.0)
        difference = rotate(partner - signal, jnp.cos(angle_set), jnp.sin(angle_set))
        signal = jnp.where(is_upper, difference, signal + partner)
    return signal


def butterfly_up(signal, az_place, bit_count):
    for bit_num in range(bit_count):
        half_span = 1 << bit_num
        partner = partner_2(signal, "az", bit_num)
        is_upper = az_place >> bit_num & 1 == 1
        angle_set = angles(az_place % half_span, 2 * half_span, 1.0)
        cosine = jnp.cos(angle_set)
        sine_part = jnp.sin(angle_set)
        lower_new = (signal + rotate(partner, cosine, sine_part)) * 0.5
        upper_new = (partner - rotate(signal, cosine, sine_part)) * 0.5
        signal = jnp.where(is_upper, upper_new, lower_new)
    return signal


def shards(raw_re, raw_im, ref_blocks, owners, offsets, taps):
    rg_cols = raw_re.shape[0]
    az_rows = raw_re.shape[1]
    az_count = lax.axis_size("az")
    az_place = lax.axis_index("az")
    bit_count = az_count.bit_length() - 1
    az_total = az_rows * az_count
    rg_total = rg_cols * lax.axis_size("rg")
    own_block = ref_blocks[0]
    lower_ref = from_root(own_block, "az", owners[0])
    upper_ref = from_root(own_block, "az", owners[1])
    signal = jnp.stack([raw_re, raw_im])
    signal = butterfly_down(signal, az_place, bit_count)
    column = jnp.zeros((), jnp.int32)
    for bit_num in range(bit_count):
        column = column + ((az_place >> bit_num & 1) << bit_count - 1 - bit_num)
    row_index = jnp.arange(az_rows, dtype=jnp.int32)
    twist = angles(row_index * column % az_total, az_total, -1.0)
    signal = rotate(signal, jnp.cos(twist)[None, :], jnp.sin(twist)[None, :])
    signal = local_dft(signal, -1.0)
    frequency = column + az_count * row_index
    signed = (frequency + az_total // 2) % az_total - az_total // 2
    az_freq = signed.astype(jnp.float32) / az_total
    rg_index = lax.axis_index("rg") * rg_cols + jnp.arange(rg_cols, dtype=jnp.int32)
    rg_freq = (rg_index.astype(jnp.float32) + 0.5) / (2 * rg_total) - 0.25
    model_phase = PHASE_GAIN * jnp.sqrt((1.0 + rg_freq)[:, None] ** 2 - az_freq[None, :] ** 2)
    ref_rows = own_block.shape[0]
    coarse = frequency * ref_rows // az_total
    slot_index = jnp.where(signed >= 0, ref_rows + coarse, coarse)
    one_hot = (jnp.arange(2 * ref_rows, dtype=jnp.int32)[:, None] == slot_index[None, :]).astype(
        jnp.float32
    )
    both_refs = jnp.concatenate([lower_ref, upper_ref], axis=0)
    picked = jnp.dot(both_refs.T, one_hot, precision=PRECISE)
    phase_all = model_phase + picked
    signal = rotate(signal, jnp.cos(phase_all), jnp.sin(phase_all))
    rim_width = REACH + TAPS // 2
    padded = padded_2(signal, (("rg", 1),), rim_width)
    offset_cols = jnp.repeat(offsets, BLOCK)
    local_cols = jnp.arange(rg_cols, dtype=jnp.int32)
    tap_index = jnp.arange(TAPS, dtype=jnp.int32)
    target = local_cols[:, None] + rim_width + offset_cols[:, None] + tap_index[None, :] - TAPS // 2
    padded_index = jnp.arange(rg_cols + 2 * rim_width, dtype=jnp.int32)
    hits = (padded_index[:, None, None] == target[None, :, :]).astype(jnp.float32)
    band_matrix = jnp.sum(hits * taps[None, :, :], axis=2)
    signal = jnp.einsum("zma,mi->zia", padded, band_matrix, precision=PRECISE)
    signal = local_dft(signal, 1.0) / az_rows
    twist_back = angles(row_index * column % az_total, az_total, 1.0)
    signal = rotate(signal, jnp.cos(twist_back)[None, :], jnp.sin(twist_back)[None, :])
    signal = butterfly_up(signal, az_place, bit_count)
    return (signal[0], signal[1])


LANES = 128
MESH = pl.DeviceIdType.MESH
RIM = REACH + TAPS // 2
TWO_PI_HI = 6.28125
TWO_PI_LO = 2.0 * math.pi - TWO_PI_HI


def split_np(matrix):
    high = matrix.astype(np.float32).astype(ml_dtypes.bfloat16)
    low = (matrix - high.astype(np.float64)).astype(np.float32).astype(ml_dtypes.bfloat16)
    return np.stack([high, low])


def tables(az_count):
    inner = LANES // az_count
    grid = np.arange(LANES)
    angle = 2.0 * np.pi * (np.outer(grid, grid) % LANES) / LANES
    cos, sin = np.cos(angle), -np.sin(angle)
    forward = [[cos, -sin], [sin, cos]]
    inverse = [[cos, sin], [-sin, cos]]
    order = np.arange(2 * LANES).reshape(2, az_count, inner).transpose(1, 0, 2).reshape(-1)
    left_in = np.block(forward)[:, order]
    right_in = np.block([[forward[o][c].T for o in range(2)] for c in range(2)])
    right_out = np.block([[inverse[o][c].T for o in range(2)] for c in range(2)])
    left_out = np.block(inverse)[order, :] / (LANES * LANES)
    matrices = np.stack([split_np(m) for m in (left_in, right_in, right_out, left_out)])
    turn = 2.0 * np.pi * np.outer(grid, grid) / (LANES * LANES)
    twiddle = np.stack([np.cos(turn), -np.sin(turn)]).astype(np.float32)
    return matrices, twiddle


def split(value):
    high = value.astype(jnp.bfloat16)
    low = (value - high.astype(jnp.float32)).astype(jnp.bfloat16)
    return high, low


def dot(a, b):
    return jnp.dot(a, b, preferred_element_type=jnp.float32)


def left_apply(table, value):
    high, low = split(value)
    return dot(table[0], high) + (dot(table[0], low) + dot(table[1], high))


def right_apply(value, table):
    high, low = split(value)
    return dot(high, table[0]) + (dot(low, table[0]) + dot(high, table[1]))


def cos_sin(phase):
    turns = jnp.floor(phase * (0.5 / math.pi) + 0.5)
    rest = (phase - turns * TWO_PI_HI) - turns * TWO_PI_LO
    half = rest * 0.5
    square = half * half
    sine = jnp.full_like(square, -1.0 / math.factorial(11))
    for power in (9, 7, 5, 3, 1):
        sine = sine * square + (-1.0) ** (power // 2) / math.factorial(power)
    sine = sine * half
    cosine = jnp.full_like(square, 1.0 / math.factorial(12))
    for power in (10, 8, 6, 4, 2, 0):
        cosine = cosine * square + (-1.0) ** (power // 2) / math.factorial(power)
    return 1.0 - 2.0 * sine * sine, 2.0 * sine * cosine


def focus_kernel(
    az_count,
    raw_re,
    raw_im,
    refs,
    owners,
    offsets,
    taps,
    matrices_hbm,
    twiddle_hbm,
    out_re,
    out_im,
    matrices,
    twiddle,
    outgoing,
    incoming,
    ref_out,
    ref_in,
    filt,
    focused,
    band,
    weigh,
    const_sem,
    ref_send,
    ref_recv,
    in_send,
    in_recv,
    back_send,
    back_recv,
    rim_send,
    rim_recv,
):
    rows = raw_re.shape[0]
    inner = raw_re.shape[1] // LANES
    piece = 2 * inner
    steps = rows // az_count
    depth = band.shape[0] // piece
    me = lax.axis_index("az")
    core = lax.axis_index("rg")
    peers = [lax.rem(me + s, az_count) for s in range(1, az_count)]
    sources = [lax.rem(me + az_count - s, az_count) for s in range(1, az_count)]
    sibling = 1 - core

    barrier = pltpu.get_barrier_semaphore()
    for peer in peers:
        pl.semaphore_signal(barrier, inc=1, device_id={"az": peer}, device_id_type=MESH)
    pl.semaphore_signal(barrier, inc=1, device_id={"rg": sibling}, device_id_type=MESH)
    load_matrices = pltpu.make_async_copy(matrices_hbm, matrices, const_sem.at[0])
    load_twiddle = pltpu.make_async_copy(twiddle_hbm, twiddle, const_sem.at[1])
    load_matrices.start()
    load_twiddle.start()

    groups = [s + (1 - core) * (steps - 1 - 2 * s) for s in range(steps)]

    def at(start, count):
        return pl.ds(start * piece if isinstance(start, int) else pl.multiple_of(start * piece, piece), count * piece)

    for comp, raw in enumerate((raw_re, raw_im)):
        for i in range(inner):
            outgoing[pl.ds(comp * inner + i, rows, stride=piece), :] = raw[:, i * LANES : (i + 1) * LANES]

    ref_rows = refs.shape[1]
    slot = lax.broadcasted_iota(jnp.int32, (depth, rows), 0)
    target = lax.broadcasted_iota(jnp.int32, (depth, rows), 1)
    target_block = target // BLOCK
    for block in range(rows // BLOCK):
        target = jnp.where(target_block == block, target + offsets[block], target)
    weights = jnp.zeros((depth, rows), jnp.float32)
    for tap in range(TAPS):
        weights = weights + jnp.where(slot == target + (RIM + tap - TAPS // 2), taps[tap : tap + 1, :], 0.0)
    high, low = split(weights.T)
    weigh[...] = jnp.concatenate([high, high, low], axis=1)
    coarse = lax.broadcasted_iota(jnp.int32, (ref_rows, LANES), 0)
    column = lax.broadcasted_iota(jnp.int32, (ref_rows, LANES), 1)
    spread = (coarse == column // (LANES // ref_rows)).astype(jnp.float32)
    wide = jnp.dot(refs[...], spread, precision=PRECISE, preferred_element_type=jnp.float32)
    ref_out[...] = jnp.zeros_like(ref_out)
    for dest in range(az_count):
        for group in range(steps):
            row = group * az_count + dest
            ref_out[dest, group : group + 1, :] = wide[row : row + 1, :]

    pl.semaphore_wait(barrier, az_count)

    def ref_copy(s, peer, source):
        return pltpu.make_async_remote_copy(
            src_ref=ref_out.at[peer],
            dst_ref=ref_in.at[source],
            send_sem=ref_send.at[s],
            recv_sem=ref_recv.at[source],
            device_id={"az": peer},
            device_id_type=MESH,
        )

    def in_copy(step, s, peer, source):
        return pltpu.make_async_remote_copy(
            src_ref=outgoing.at[at(groups[step] * az_count + peer, 1), :],
            dst_ref=incoming.at[at(groups[step] * az_count + source, 1), :],
            send_sem=in_send.at[step, s],
            recv_sem=in_recv.at[step, source],
            device_id={"az": peer},
            device_id_type=MESH,
        )

    def back_copy(step, s, peer, source):
        return pltpu.make_async_remote_copy(
            src_ref=focused.at[at(groups[step] * az_count + peer, 1), :],
            dst_ref=band.at[at(RIM + groups[step] * az_count + source, 1), :],
            send_sem=back_send.at[step, s],
            recv_sem=back_recv.at[step, source],
            device_id={"az": peer},
            device_id_type=MESH,
        )

    def rim_copy(step):
        count = (az_count, RIM - az_count)[step]
        first = ((rows - az_count, rows - RIM)[step], (0, az_count)[step])
        place = ((RIM - az_count, 0)[step], (RIM + rows, RIM + rows + az_count)[step])
        return pltpu.make_async_remote_copy(
            src_ref=band.at[at(RIM + first[0] * (1 - core) + first[1] * core, count), :],
            dst_ref=band.at[at(place[0] * (1 - core) + place[1] * core, count), :],
            send_sem=rim_send.at[step],
            recv_sem=rim_recv.at[step],
            device_id={"rg": sibling},
            device_id_type=MESH,
        )

    def rim_arrival(step):
        count = (az_count, RIM - az_count)[step]
        place = ((RIM - az_count, 0)[step], (RIM + rows, RIM + rows + az_count)[step])
        return pltpu.make_async_remote_copy(
            src_ref=band.at[at(RIM, count), :],
            dst_ref=band.at[at(place[0] * core + place[1] * (1 - core), count), :],
            send_sem=rim_send.at[step],
            recv_sem=rim_recv.at[step],
            device_id={"rg": sibling},
            device_id_type=MESH,
        )

    for s, peer in enumerate(peers):
        ref_copy(s, peer, me).start()
    for step in range(steps):
        for s, peer in enumerate(peers):
            in_copy(step, s, peer, me).start()

    for group in range(steps):
        own = at(group * az_count + me, 1)
        incoming[own, :] = outgoing[own, :]
    ref_in[me] = ref_out[me]
    band[at((RIM + rows) * core, RIM), :] = jnp.zeros((RIM * piece, LANES), jnp.float32)
    spare = depth - rows - 2 * RIM
    band[at(depth - spare, spare), :] = jnp.zeros((spare * piece, LANES), jnp.float32)

    for s, source in enumerate(sources):
        ref_copy(s, peers[s], source).wait_recv()
    lane = lax.broadcasted_iota(jnp.int32, ref_in.shape[1:], 1)
    picked = jnp.zeros(ref_in.shape[1:], jnp.float32)
    for source in range(az_count):
        wanted = jnp.where(lane < LANES // 2, owners[1], owners[0]) == source
        picked = jnp.where(wanted, ref_in[source], picked)
    az_total = LANES * LANES
    low = lax.broadcasted_iota(jnp.int32, (LANES, LANES), 0)
    high = lax.broadcasted_iota(jnp.int32, (LANES, LANES), 1)
    frequency = low + LANES * high
    signed = jnp.where(frequency >= az_total // 2, frequency - az_total, frequency)
    az_freq = signed.astype(jnp.float32) / az_total
    az_square = az_freq * az_freq
    for group in range(steps):
        index = core * rows + group * az_count + me
        rg_freq = 1.0 + ((index.astype(jnp.float32) + 0.5) * (1.0 / (4 * rows)) - 0.25)
        phase = PHASE_GAIN * jnp.sqrt(rg_freq * rg_freq - az_square) + picked[group : group + 1, :]
        cosine, sine = cos_sin(phase)
        filt[group, 0] = cosine
        filt[group, 1] = sine

    load_matrices.wait()
    load_twiddle.wait()
    for step in range(steps):
        group = groups[step]
        for s, source in enumerate(sources):
            in_copy(step, s, peers[s], source).wait_recv()
        whole = at(group * az_count, az_count)
        value = left_apply((matrices[0, 0], matrices[0, 1]), incoming[whole, :])
        cosine, sine = twiddle[0], twiddle[1]
        real, imag = value[:LANES], value[LANES:]
        value = jnp.concatenate([real * cosine - imag * sine, real * sine + imag * cosine], axis=1)
        value = right_apply(value, (matrices[1, 0], matrices[1, 1]))
        real, imag = value[:, :LANES], value[:, LANES:]
        cosine, sine = filt[group, 0], filt[group, 1]
        value = jnp.concatenate([real * cosine - imag * sine, real * sine + imag * cosine], axis=1)
        value = right_apply(value, (matrices[2, 0], matrices[2, 1]))
        real, imag = value[:, :LANES], value[:, LANES:]
        cosine, sine = twiddle[0], twiddle[1]
        value = jnp.concatenate([real * cosine + imag * sine, imag * cosine - real * sine], axis=0)
        focused[whole, :] = left_apply((matrices[3, 0], matrices[3, 1]), value)
        for s, peer in enumerate(peers):
            back_copy(step, s, peer, me).start()
        band[at(RIM + group * az_count + me, 1), :] = focused[at(group * az_count + me, 1), :]
        if step >= steps - 2:
            early = step - (steps - 2)
            for s, source in enumerate(sources):
                back_copy(early, s, peers[s], source).wait_recv()
            rim_copy(early).start()
    for step in range(2, steps):
        for s, source in enumerate(sources):
            back_copy(step, s, peers[s], source).wait_recv()
    for step in range(2):
        rim_arrival(step).wait_recv()

    weights = weigh[...]
    pair = 2 * LANES
    for comp, out in enumerate((out_re, out_im)):
        for i in range(0, inner, 2):
            value = jnp.concatenate(
                [band[pl.ds(comp * inner + i + j, depth, stride=piece), :] for j in range(2)], axis=1
            )
            high, low = split(value)
            value = dot(weights, jnp.concatenate([high, low, high], axis=0))
            out[:, i * LANES : i * LANES + pair] = value

    for s, peer in enumerate(peers):
        ref_copy(s, peer, me).wait_send()
        for step in range(steps):
            in_copy(step, s, peer, me).wait_send()
            back_copy(step, s, peer, me).wait_send()
    for step in range(2):
        rim_copy(step).wait_send()


def fused_shards(az_count, raw_re, raw_im, ref_blocks, owners, offsets, taps):
    rows, samples = raw_re.shape
    piece = 2 * samples // LANES
    steps = rows // az_count
    depth = -(-(rows + 2 * RIM) // 16) * 16
    matrices, twiddle = tables(az_count)
    vmem = pl.BlockSpec(memory_space=pltpu.VMEM)
    smem = pl.BlockSpec(memory_space=pltpu.SMEM)
    anywhere = pl.BlockSpec(memory_space=pl.ANY)
    dma = pltpu.SemaphoreType.DMA
    flat = pltpu.VMEM((rows * piece, LANES), jnp.float32)
    return pl.pallas_call(
        functools.partial(focus_kernel, az_count),
        out_shape=[jax.ShapeDtypeStruct(raw_re.shape, jnp.float32)] * 2,
        in_specs=[vmem, vmem, vmem, smem, smem, vmem, anywhere, anywhere],
        out_specs=[vmem, vmem],
        scratch_shapes=[
            pltpu.VMEM(matrices.shape, jnp.bfloat16),
            pltpu.VMEM(twiddle.shape, jnp.float32),
            flat,
            flat,
            pltpu.VMEM((az_count, 8, LANES), jnp.float32),
            pltpu.VMEM((az_count, 8, LANES), jnp.float32),
            pltpu.VMEM((steps, 2, LANES, LANES), jnp.float32),
            flat,
            pltpu.VMEM((depth * piece, LANES), jnp.float32),
            pltpu.VMEM((rows, 3 * depth), jnp.bfloat16),
            dma((2,)),
            dma((az_count,)),
            dma((az_count,)),
            dma((steps, az_count)),
            dma((steps, az_count)),
            dma((steps, az_count)),
            dma((steps, az_count)),
            dma((2,)),
            dma((2,)),
        ],
        compiler_params=pltpu.CompilerParams(
            collective_id=0, has_side_effects=True, vmem_limit_bytes=32 * 1024 * 1024
        ),
    )(raw_re, raw_im, ref_blocks[0].T, owners, offsets, taps.T, jnp.asarray(matrices), jnp.asarray(twiddle))


def body_for(mesh):
    az_count, rg_count = mesh.shape["az"], mesh.shape["rg"]

    def body(raw_re, raw_im, ref_blocks, owners, offsets, taps):
        rows, samples = raw_re.shape
        fits = (
            samples * az_count == LANES * LANES
            and az_count == 8
            and rows == 4 * az_count
            and rg_count == 2
            and ref_blocks.shape[1] == 64
        )
        if fits:
            return tuple(fused_shards(az_count, raw_re, raw_im, ref_blocks, owners, offsets, taps))
        return shards(raw_re, raw_im, ref_blocks, owners, offsets, taps)

    return body


def solution(mesh):
    return jax.shard_map(
        body_for(mesh),
        mesh=mesh,
        in_specs=(
            P("rg", ("scene", "az")),
            P("rg", ("scene", "az")),
            P(("scene", "az"), None, "rg"),
            P("scene"),
            P("rg"),
            P("rg", None),
        ),
        out_specs=(P("rg", ("scene", "az")), P("rg", ("scene", "az"))),
        check_vma=False,
    )
```

```python
import functools
import math

import jax
import jax.numpy as jnp
import ml_dtypes
import numpy as np
from jax import lax
from jax.experimental import pallas as pl
from jax.experimental.pallas import tpu as pltpu
from jax.sharding import PartitionSpec as P

SPLIT = 4
TAPS = 8
REACH = 8
BLOCK = 16


PRECISE = lax.Precision.HIGHEST
PHASE_GAIN = 50.0


def partner_2(value, axis, stride):
    return lax.ppermute(value, axis, [(i, i ^ 1 << stride) for i in range(lax.axis_size(axis))])


def from_root(block, axis, source):
    block = jnp.where(lax.axis_index(axis) == source, block, jnp.zeros_like(block))
    return lax.psum(block, axis)


def padded_2(value, sides, width):
    for axis, dim in sides:
        size, length = (lax.axis_size(axis), value.shape[dim])
        up = [(i, (i + 1) % size) for i in range(size - 1)]
        down = [(j, i) for i, j in up]
        last = lax.slice_in_dim(value, length - width, length, axis=dim)
        initial = lax.slice_in_dim(value, 0, width, axis=dim)
        before = lax.ppermute(last, axis, up)
        after = lax.ppermute(initial, axis, down)
        value = jnp.concatenate([before, value, after], axis=dim)
    return value


def angles(numerator, denominator, sign_value):
    return sign_value * 2.0 * math.pi * numerator.astype(jnp.float32) / denominator


def rotate(signal, cosine, sine_part):
    real_part = signal[0] * cosine - signal[1] * sine_part
    imag_part = signal[0] * sine_part + signal[1] * cosine
    return jnp.stack([real_part, imag_part])


def dft_table(length_n, sign_value):
    counter = jnp.arange(length_n, dtype=jnp.int32)
    turn_count = counter[:, None] * counter[None, :] % length_n
    angle_set = angles(turn_count, length_n, sign_value)
    return (jnp.cos(angle_set), jnp.sin(angle_set))


def complex_apply(einsum_form, cosine, sine_part, signal):
    real_part = jnp.einsum(einsum_form, cosine, signal[0], precision=PRECISE) - jnp.einsum(
        einsum_form, sine_part, signal[1], precision=PRECISE
    )
    imag_part = jnp.einsum(einsum_form, cosine, signal[1], precision=PRECISE) + jnp.einsum(
        einsum_form, sine_part, signal[0], precision=PRECISE
    )
    return jnp.stack([real_part, imag_part])


def local_dft(signal, sign_value):
    rg_cols = signal.shape[1]
    az_rows = signal.shape[2]
    inner_len = az_rows // SPLIT
    shaped = signal.reshape(2, rg_cols, SPLIT, inner_len)
    first_cos, first_sin = dft_table(SPLIT, sign_value)
    first_pass = complex_apply("aj,cjk->cak", first_cos, first_sin, shaped)
    outer_idx = jnp.arange(SPLIT, dtype=jnp.int32)
    inner_idx = jnp.arange(inner_len, dtype=jnp.int32)
    twist = angles(outer_idx[:, None] * inner_idx[None, :] % az_rows, az_rows, sign_value)
    first_pass = rotate(first_pass, jnp.cos(twist)[None, :, :], jnp.sin(twist)[None, :, :])
    second_cos, second_sin = dft_table(inner_len, sign_value)
    second_pass = complex_apply("bk,cak->cba", second_cos, second_sin, first_pass)
    return second_pass.reshape(2, rg_cols, az_rows)


def butterfly_down(signal, az_place, bit_count):
    for bit_num in reversed(range(bit_count)):
        half_span = 1 << bit_num
        partner = partner_2(signal, "az", bit_num)
        is_upper = az_place >> bit_num & 1 == 1
        angle_set = angles(az_place % half_span, 2 * half_span, -1.0)
        difference = rotate(partner - signal, jnp.cos(angle_set), jnp.sin(angle_set))
        signal = jnp.where(is_upper, difference, signal + partner)
    return signal


def butterfly_up(signal, az_place, bit_count):
    for bit_num in range(bit_count):
        half_span = 1 << bit_num
        partner = partner_2(signal, "az", bit_num)
        is_upper = az_place >> bit_num & 1 == 1
        angle_set = angles(az_place % half_span, 2 * half_span, 1.0)
        cosine = jnp.cos(angle_set)
        sine_part = jnp.sin(angle_set)
        lower_new = (signal + rotate(partner, cosine, sine_part)) * 0.5
        upper_new = (partner - rotate(signal, cosine, sine_part)) * 0.5
        signal = jnp.where(is_upper, upper_new, lower_new)
    return signal


def shards(raw_re, raw_im, ref_blocks, owners, offsets, taps):
    rg_cols = raw_re.shape[0]
    az_rows = raw_re.shape[1]
    az_count = lax.axis_size("az")
    az_place = lax.axis_index("az")
    bit_count = az_count.bit_length() - 1
    az_total = az_rows * az_count
    rg_total = rg_cols * lax.axis_size("rg")
    own_block = ref_blocks[0]
    lower_ref = from_root(own_block, "az", owners[0])
    upper_ref = from_root(own_block, "az", owners[1])
    signal = jnp.stack([raw_re, raw_im])
    signal = butterfly_down(signal, az_place, bit_count)
    column = jnp.zeros((), jnp.int32)
    for bit_num in range(bit_count):
        column = column + ((az_place >> bit_num & 1) << bit_count - 1 - bit_num)
    row_index = jnp.arange(az_rows, dtype=jnp.int32)
    twist = angles(row_index * column % az_total, az_total, -1.0)
    signal = rotate(signal, jnp.cos(twist)[None, :], jnp.sin(twist)[None, :])
    signal = local_dft(signal, -1.0)
    frequency = column + az_count * row_index
    signed = (frequency + az_total // 2) % az_total - az_total // 2
    az_freq = signed.astype(jnp.float32) / az_total
    rg_index = lax.axis_index("rg") * rg_cols + jnp.arange(rg_cols, dtype=jnp.int32)
    rg_freq = (rg_index.astype(jnp.float32) + 0.5) / (2 * rg_total) - 0.25
    model_phase = PHASE_GAIN * jnp.sqrt((1.0 + rg_freq)[:, None] ** 2 - az_freq[None, :] ** 2)
    ref_rows = own_block.shape[0]
    coarse = frequency * ref_rows // az_total
    slot_index = jnp.where(signed >= 0, ref_rows + coarse, coarse)
    one_hot = (jnp.arange(2 * ref_rows, dtype=jnp.int32)[:, None] == slot_index[None, :]).astype(
        jnp.float32
    )
    both_refs = jnp.concatenate([lower_ref, upper_ref], axis=0)
    picked = jnp.dot(both_refs.T, one_hot, precision=PRECISE)
    phase_all = model_phase + picked
    signal = rotate(signal, jnp.cos(phase_all), jnp.sin(phase_all))
    rim_width = REACH + TAPS // 2
    padded = padded_2(signal, (("rg", 1),), rim_width)
    offset_cols = jnp.repeat(offsets, BLOCK)
    local_cols = jnp.arange(rg_cols, dtype=jnp.int32)
    tap_index = jnp.arange(TAPS, dtype=jnp.int32)
    target = local_cols[:, None] + rim_width + offset_cols[:, None] + tap_index[None, :] - TAPS // 2
    padded_index = jnp.arange(rg_cols + 2 * rim_width, dtype=jnp.int32)
    hits = (padded_index[:, None, None] == target[None, :, :]).astype(jnp.float32)
    band_matrix = jnp.sum(hits * taps[None, :, :], axis=2)
    signal = jnp.einsum("zma,mi->zia", padded, band_matrix, precision=PRECISE)
    signal = local_dft(signal, 1.0) / az_rows
    twist_back = angles(row_index * column % az_total, az_total, 1.0)
    signal = rotate(signal, jnp.cos(twist_back)[None, :], jnp.sin(twist_back)[None, :])
    signal = butterfly_up(signal, az_place, bit_count)
    return (signal[0], signal[1])


LANES = 128
MESH = pl.DeviceIdType.MESH
RIM = REACH + TAPS // 2
TWO_PI_HI = 6.28125
TWO_PI_LO = 2.0 * math.pi - TWO_PI_HI


def split_np(matrix):
    high = matrix.astype(np.float32).astype(ml_dtypes.bfloat16)
    low = (matrix - high.astype(np.float64)).astype(np.float32).astype(ml_dtypes.bfloat16)
    return np.stack([high, low])


def tables(az_count):
    inner = LANES // az_count
    grid = np.arange(LANES)
    angle = 2.0 * np.pi * (np.outer(grid, grid) % LANES) / LANES
    cos, sin = np.cos(angle), -np.sin(angle)
    forward = [[cos, -sin], [sin, cos]]
    inverse = [[cos, sin], [-sin, cos]]
    order = np.arange(2 * LANES).reshape(2, az_count, inner).transpose(1, 0, 2).reshape(-1)
    left_in = np.block(forward)[:, order]
    right_in = np.block([[forward[o][c].T for o in range(2)] for c in range(2)])
    right_out = np.block([[inverse[o][c].T for o in range(2)] for c in range(2)])
    left_out = np.block(inverse)[order, :] / (LANES * LANES)
    matrices = np.stack([split_np(m) for m in (left_in, right_in, right_out, left_out)])
    turn = 2.0 * np.pi * np.outer(grid, grid) / (LANES * LANES)
    twiddle = np.stack([np.cos(turn), -np.sin(turn)]).astype(np.float32)
    return matrices, twiddle


def split(value):
    high = value.astype(jnp.bfloat16)
    low = (value - high.astype(jnp.float32)).astype(jnp.bfloat16)
    return high, low


def dot(a, b):
    return jnp.dot(a, b, preferred_element_type=jnp.float32)


def left_apply(table, value):
    high, low = split(value)
    return dot(table[0], high) + (dot(table[0], low) + dot(table[1], high))


def right_apply(value, table):
    high, low = split(value)
    return dot(high, table[0]) + (dot(low, table[0]) + dot(high, table[1]))


def cos_sin(phase):
    turns = jnp.floor(phase * (0.5 / math.pi) + 0.5)
    rest = (phase - turns * TWO_PI_HI) - turns * TWO_PI_LO
    half = rest * 0.5
    square = half * half
    sine = jnp.full_like(square, -1.0 / math.factorial(11))
    for power in (9, 7, 5, 3, 1):
        sine = sine * square + (-1.0) ** (power // 2) / math.factorial(power)
    sine = sine * half
    cosine = jnp.full_like(square, 1.0 / math.factorial(12))
    for power in (10, 8, 6, 4, 2, 0):
        cosine = cosine * square + (-1.0) ** (power // 2) / math.factorial(power)
    return 1.0 - 2.0 * sine * sine, 2.0 * sine * cosine


def focus_kernel(
    az_count,
    re_hbm,
    im_hbm,
    refs_hbm,
    owners,
    offsets,
    taps_hbm,
    matrices_hbm,
    twiddle_hbm,
    out_re,
    out_im,
    raw,
    refs,
    taps,
    matrices,
    twiddle,
    outgoing,
    incoming,
    ref_out,
    ref_in,
    filt,
    focused,
    band,
    weigh,
    raw_sem,
    const_sem,
    ref_send,
    ref_recv,
    in_send,
    in_recv,
    back_send,
    back_recv,
    rim_send,
    rim_recv,
):
    rows = re_hbm.shape[0]
    inner = re_hbm.shape[1] // LANES
    piece = 2 * inner
    steps = rows // az_count
    depth = band.shape[0] // piece
    me = lax.axis_index("az")
    core = lax.axis_index("rg")
    peers = []
    for flips in sorted(range(1, az_count), reverse=True):
        peer = me
        for bit in (1 << b for b in range(az_count.bit_length())):
            if flips & bit:
                peer = peer + bit - 2 * bit * lax.rem(lax.div(peer, bit), 2)
        peers.append(peer)
    sources = peers
    sibling = 1 - core
    groups = [s + (1 - core) * (steps - 1 - 2 * s) for s in range(steps)]

    def raw_copy(step, comp):
        group = pl.ds(pl.multiple_of(groups[step] * az_count, az_count), az_count)
        hbm = (re_hbm, im_hbm)[comp]
        return pltpu.make_async_copy(hbm.at[group, :], raw.at[comp, step], raw_sem.at[step, comp])

    load_refs = pltpu.make_async_copy(refs_hbm, refs, const_sem.at[2])
    load_taps = pltpu.make_async_copy(taps_hbm, taps, const_sem.at[3])
    load_refs.start()
    for step in range(steps):
        for comp in range(2):
            raw_copy(step, comp).start()

    barrier = pltpu.get_barrier_semaphore()
    for peer in peers:
        pl.semaphore_signal(barrier, inc=1, device_id={"az": peer}, device_id_type=MESH)
    pl.semaphore_signal(barrier, inc=1, device_id={"rg": sibling}, device_id_type=MESH)
    load_matrices = pltpu.make_async_copy(matrices_hbm, matrices, const_sem.at[0])
    load_twiddle = pltpu.make_async_copy(twiddle_hbm, twiddle, const_sem.at[1])
    load_matrices.start()
    load_twiddle.start()
    load_taps.start()

    def at(start, count):
        return pl.ds(start * piece if isinstance(start, int) else pl.multiple_of(start * piece, piece), count * piece)

    ref_rows = refs.shape[1]
    coarse = lax.broadcasted_iota(jnp.int32, (ref_rows, LANES), 0)
    column = lax.broadcasted_iota(jnp.int32, (ref_rows, LANES), 1)
    spread = (coarse == column // (LANES // ref_rows)).astype(jnp.float32)
    load_refs.wait()
    wide = jnp.dot(refs[...], spread, precision=PRECISE, preferred_element_type=jnp.float32)
    ref_out[...] = jnp.zeros_like(ref_out)
    for dest in range(az_count):
        for group in range(steps):
            row = group * az_count + dest
            ref_out[dest, group : group + 1, :] = wide[row : row + 1, :]

    def ref_copy(s, peer, source):
        return pltpu.make_async_remote_copy(
            src_ref=ref_out.at[peer],
            dst_ref=ref_in.at[source],
            send_sem=ref_send.at[s],
            recv_sem=ref_recv.at[source],
            device_id={"az": peer},
            device_id_type=MESH,
        )

    def in_copy(step, s, peer, source):
        return pltpu.make_async_remote_copy(
            src_ref=outgoing.at[at(groups[step] * az_count + peer, 1), :],
            dst_ref=incoming.at[at(groups[step] * az_count + source, 1), :],
            send_sem=in_send.at[step, s],
            recv_sem=in_recv.at[step, source],
            device_id={"az": peer},
            device_id_type=MESH,
        )

    def back_copy(step, s, peer, source):
        return pltpu.make_async_remote_copy(
            src_ref=focused.at[at(groups[step] * az_count + peer, 1), :],
            dst_ref=band.at[at(RIM + groups[step] * az_count + source, 1), :],
            send_sem=back_send.at[step, s],
            recv_sem=back_recv.at[step, source],
            device_id={"az": peer},
            device_id_type=MESH,
        )

    def rim_copy(step):
        count = (az_count, RIM - az_count)[step]
        first = ((rows - az_count, rows - RIM)[step], (0, az_count)[step])
        place = ((RIM - az_count, 0)[step], (RIM + rows, RIM + rows + az_count)[step])
        return pltpu.make_async_remote_copy(
            src_ref=band.at[at(RIM + first[0] * (1 - core) + first[1] * core, count), :],
            dst_ref=band.at[at(place[0] * (1 - core) + place[1] * core, count), :],
            send_sem=rim_send.at[step],
            recv_sem=rim_recv.at[step],
            device_id={"rg": sibling},
            device_id_type=MESH,
        )

    def rim_arrival(step):
        count = (az_count, RIM - az_count)[step]
        place = ((RIM - az_count, 0)[step], (RIM + rows, RIM + rows + az_count)[step])
        return pltpu.make_async_remote_copy(
            src_ref=band.at[at(RIM, count), :],
            dst_ref=band.at[at(place[0] * core + place[1] * (1 - core), count), :],
            send_sem=rim_send.at[step],
            recv_sem=rim_recv.at[step],
            device_id={"rg": sibling},
            device_id_type=MESH,
        )

    for step in range(steps):
        for comp in range(2):
            raw_copy(step, comp).wait()
            for i in range(inner):
                place = groups[step] * (az_count * piece) + (comp * inner + i)
                outgoing[pl.ds(place, az_count, stride=piece), :] = raw[comp, step, :, i * LANES : (i + 1) * LANES]
        if step == 0:
            pl.semaphore_wait(barrier, az_count)
            for s, peer in enumerate(peers):
                ref_copy(s, peer, me).start()
        for s, peer in enumerate(peers):
            in_copy(step, s, peer, me).start()
        own = at(groups[step] * az_count + me, 1)
        incoming[own, :] = outgoing[own, :]

    load_taps.wait()
    slot = lax.broadcasted_iota(jnp.int32, (depth, rows), 0)
    target = lax.broadcasted_iota(jnp.int32, (depth, rows), 1)
    target_block = target // BLOCK
    for block in range(rows // BLOCK):
        target = jnp.where(target_block == block, target + offsets[block], target)
    weights = jnp.zeros((depth, rows), jnp.float32)
    for tap in range(TAPS):
        weights = weights + jnp.where(slot == target + (RIM + tap - TAPS // 2), taps[tap : tap + 1, :], 0.0)
    high, low = split(weights.T)
    weigh[...] = jnp.concatenate([high, high, low], axis=1)

    ref_in[me] = ref_out[me]
    band[at((RIM + rows) * core, RIM), :] = jnp.zeros((RIM * piece, LANES), jnp.float32)
    spare = depth - rows - 2 * RIM
    band[at(depth - spare, spare), :] = jnp.zeros((spare * piece, LANES), jnp.float32)

    for s, source in enumerate(sources):
        ref_copy(s, peers[s], source).wait_recv()
    lane = lax.broadcasted_iota(jnp.int32, ref_in.shape[1:], 1)
    picked = jnp.zeros(ref_in.shape[1:], jnp.float32)
    for source in range(az_count):
        wanted = jnp.where(lane < LANES // 2, owners[1], owners[0]) == source
        picked = jnp.where(wanted, ref_in[source], picked)
    az_total = LANES * LANES
    low = lax.broadcasted_iota(jnp.int32, (LANES, LANES), 0)
    high = lax.broadcasted_iota(jnp.int32, (LANES, LANES), 1)
    frequency = low + LANES * high
    signed = jnp.where(frequency >= az_total // 2, frequency - az_total, frequency)
    az_freq = signed.astype(jnp.float32) / az_total
    az_square = az_freq * az_freq
    for group in range(steps):
        index = core * rows + group * az_count + me
        rg_freq = 1.0 + ((index.astype(jnp.float32) + 0.5) * (1.0 / (4 * rows)) - 0.25)
        phase = PHASE_GAIN * jnp.sqrt(rg_freq * rg_freq - az_square) + picked[group : group + 1, :]
        cosine, sine = cos_sin(phase)
        filt[group, 0] = cosine
        filt[group, 1] = sine

    load_matrices.wait()
    load_twiddle.wait()
    for step in range(steps):
        group = groups[step]
        for s, source in enumerate(sources):
            in_copy(step, s, peers[s], source).wait_recv()
        whole = at(group * az_count, az_count)
        value = left_apply((matrices[0, 0], matrices[0, 1]), incoming[whole, :])
        cosine, sine = twiddle[0], twiddle[1]
        real, imag = value[:LANES], value[LANES:]
        value = jnp.concatenate([real * cosine - imag * sine, real * sine + imag * cosine], axis=1)
        value = right_apply(value, (matrices[1, 0], matrices[1, 1]))
        real, imag = value[:, :LANES], value[:, LANES:]
        cosine, sine = filt[group, 0], filt[group, 1]
        value = jnp.concatenate([real * cosine - imag * sine, real * sine + imag * cosine], axis=1)
        value = right_apply(value, (matrices[2, 0], matrices[2, 1]))
        real, imag = value[:, :LANES], value[:, LANES:]
        cosine, sine = twiddle[0], twiddle[1]
        value = jnp.concatenate([real * cosine + imag * sine, imag * cosine - real * sine], axis=0)
        focused[whole, :] = left_apply((matrices[3, 0], matrices[3, 1]), value)
        for s, peer in enumerate(peers):
            back_copy(step, s, peer, me).start()
        band[at(RIM + group * az_count + me, 1), :] = focused[at(group * az_count + me, 1), :]
        if step >= steps - 2:
            early = step - (steps - 2)
            for s, source in enumerate(sources):
                back_copy(early, s, peers[s], source).wait_recv()
            rim_copy(early).start()
    for step in range(2, steps):
        for s, source in enumerate(sources):
            back_copy(step, s, peers[s], source).wait_recv()
    for step in range(2):
        rim_arrival(step).wait_recv()

    weights = weigh[...]
    pair = 2 * LANES
    for comp, out in enumerate((out_re, out_im)):
        for i in range(0, inner, 2):
            value = jnp.concatenate(
                [band[pl.ds(comp * inner + i + j, depth, stride=piece), :] for j in range(2)], axis=1
            )
            high, low = split(value)
            value = dot(weights, jnp.concatenate([high, low, high], axis=0))
            out[:, i * LANES : i * LANES + pair] = value

    for s, peer in enumerate(peers):
        ref_copy(s, peer, me).wait_send()
        for step in range(steps):
            in_copy(step, s, peer, me).wait_send()
            back_copy(step, s, peer, me).wait_send()
    for step in range(2):
        rim_copy(step).wait_send()


def fused_shards(az_count, raw_re, raw_im, ref_blocks, owners, offsets, taps):
    rows, samples = raw_re.shape
    ref_rows = ref_blocks.shape[1]
    piece = 2 * samples // LANES
    steps = rows // az_count
    depth = -(-(rows + 2 * RIM) // 16) * 16
    matrices, twiddle = tables(az_count)
    vmem = pl.BlockSpec(memory_space=pltpu.VMEM)
    smem = pl.BlockSpec(memory_space=pltpu.SMEM)
    hbm = pl.BlockSpec(memory_space=pltpu.HBM)
    dma = pltpu.SemaphoreType.DMA
    flat = pltpu.VMEM((rows * piece, LANES), jnp.float32)
    return pl.pallas_call(
        functools.partial(focus_kernel, az_count),
        out_shape=[jax.ShapeDtypeStruct(raw_re.shape, jnp.float32)] * 2,
        in_specs=[hbm, hbm, hbm, smem, smem, hbm, hbm, hbm],
        out_specs=[vmem, vmem],
        scratch_shapes=[
            pltpu.VMEM((2, steps, az_count, samples), jnp.float32),
            pltpu.VMEM((rows, ref_rows), jnp.float32),
            pltpu.VMEM((TAPS, rows), jnp.float32),
            pltpu.VMEM(matrices.shape, jnp.bfloat16),
            pltpu.VMEM(twiddle.shape, jnp.float32),
            flat,
            flat,
            pltpu.VMEM((az_count, 8, LANES), jnp.float32),
            pltpu.VMEM((az_count, 8, LANES), jnp.float32),
            pltpu.VMEM((steps, 2, LANES, LANES), jnp.float32),
            flat,
            pltpu.VMEM((depth * piece, LANES), jnp.float32),
            pltpu.VMEM((rows, 3 * depth), jnp.bfloat16),
            dma((steps, 2)),
            dma((4,)),
            dma((az_count,)),
            dma((az_count,)),
            dma((steps, az_count)),
            dma((steps, az_count)),
            dma((steps, az_count)),
            dma((steps, az_count)),
            dma((2,)),
            dma((2,)),
        ],
        compiler_params=pltpu.CompilerParams(
            collective_id=0, has_side_effects=True, vmem_limit_bytes=62 * 1024 * 1024
        ),
    )(raw_re, raw_im, ref_blocks[0].T, owners, offsets, taps.T, jnp.asarray(matrices), jnp.asarray(twiddle))


def body_for(mesh):
    az_count, rg_count = mesh.shape["az"], mesh.shape["rg"]

    def body(raw_re, raw_im, ref_blocks, owners, offsets, taps):
        rows, samples = raw_re.shape
        fits = (
            samples * az_count == LANES * LANES
            and az_count == 8
            and rows == 4 * az_count
            and rg_count == 2
            and ref_blocks.shape[1] == 64
        )
        if fits:
            return tuple(fused_shards(az_count, raw_re, raw_im, ref_blocks, owners, offsets, taps))
        return shards(raw_re, raw_im, ref_blocks, owners, offsets, taps)

    return body


def solution(mesh):
    return jax.shard_map(
        body_for(mesh),
        mesh=mesh,
        in_specs=(
            P("rg", ("scene", "az")),
            P("rg", ("scene", "az")),
            P(("scene", "az"), None, "rg"),
            P("scene"),
            P("rg"),
            P("rg", None),
        ),
        out_specs=(P("rg", ("scene", "az")), P("rg", ("scene", "az"))),
        check_vma=False,
    )
```

```python
import functools
import math

import jax
import jax.numpy as jnp
import ml_dtypes
import numpy as np
from jax import lax
from jax.experimental import pallas as pl
from jax.experimental.pallas import tpu as pltpu
from jax.sharding import PartitionSpec as P

SPLIT = 4
TAPS = 8
REACH = 8
BLOCK = 16


PRECISE = lax.Precision.HIGHEST
PHASE_GAIN = 50.0


def partner_2(value, axis, stride):
    return lax.ppermute(value, axis, [(i, i ^ 1 << stride) for i in range(lax.axis_size(axis))])


def from_root(block, axis, source):
    block = jnp.where(lax.axis_index(axis) == source, block, jnp.zeros_like(block))
    return lax.psum(block, axis)


def padded_2(value, sides, width):
    for axis, dim in sides:
        size, length = (lax.axis_size(axis), value.shape[dim])
        up = [(i, (i + 1) % size) for i in range(size - 1)]
        down = [(j, i) for i, j in up]
        last = lax.slice_in_dim(value, length - width, length, axis=dim)
        initial = lax.slice_in_dim(value, 0, width, axis=dim)
        before = lax.ppermute(last, axis, up)
        after = lax.ppermute(initial, axis, down)
        value = jnp.concatenate([before, value, after], axis=dim)
    return value


def angles(numerator, denominator, sign_value):
    return sign_value * 2.0 * math.pi * numerator.astype(jnp.float32) / denominator


def rotate(signal, cosine, sine_part):
    real_part = signal[0] * cosine - signal[1] * sine_part
    imag_part = signal[0] * sine_part + signal[1] * cosine
    return jnp.stack([real_part, imag_part])


def dft_table(length_n, sign_value):
    counter = jnp.arange(length_n, dtype=jnp.int32)
    turn_count = counter[:, None] * counter[None, :] % length_n
    angle_set = angles(turn_count, length_n, sign_value)
    return (jnp.cos(angle_set), jnp.sin(angle_set))


def complex_apply(einsum_form, cosine, sine_part, signal):
    real_part = jnp.einsum(einsum_form, cosine, signal[0], precision=PRECISE) - jnp.einsum(
        einsum_form, sine_part, signal[1], precision=PRECISE
    )
    imag_part = jnp.einsum(einsum_form, cosine, signal[1], precision=PRECISE) + jnp.einsum(
        einsum_form, sine_part, signal[0], precision=PRECISE
    )
    return jnp.stack([real_part, imag_part])


def local_dft(signal, sign_value):
    rg_cols = signal.shape[1]
    az_rows = signal.shape[2]
    inner_len = az_rows // SPLIT
    shaped = signal.reshape(2, rg_cols, SPLIT, inner_len)
    first_cos, first_sin = dft_table(SPLIT, sign_value)
    first_pass = complex_apply("aj,cjk->cak", first_cos, first_sin, shaped)
    outer_idx = jnp.arange(SPLIT, dtype=jnp.int32)
    inner_idx = jnp.arange(inner_len, dtype=jnp.int32)
    twist = angles(outer_idx[:, None] * inner_idx[None, :] % az_rows, az_rows, sign_value)
    first_pass = rotate(first_pass, jnp.cos(twist)[None, :, :], jnp.sin(twist)[None, :, :])
    second_cos, second_sin = dft_table(inner_len, sign_value)
    second_pass = complex_apply("bk,cak->cba", second_cos, second_sin, first_pass)
    return second_pass.reshape(2, rg_cols, az_rows)


def butterfly_down(signal, az_place, bit_count):
    for bit_num in reversed(range(bit_count)):
        half_span = 1 << bit_num
        partner = partner_2(signal, "az", bit_num)
        is_upper = az_place >> bit_num & 1 == 1
        angle_set = angles(az_place % half_span, 2 * half_span, -1.0)
        difference = rotate(partner - signal, jnp.cos(angle_set), jnp.sin(angle_set))
        signal = jnp.where(is_upper, difference, signal + partner)
    return signal


def butterfly_up(signal, az_place, bit_count):
    for bit_num in range(bit_count):
        half_span = 1 << bit_num
        partner = partner_2(signal, "az", bit_num)
        is_upper = az_place >> bit_num & 1 == 1
        angle_set = angles(az_place % half_span, 2 * half_span, 1.0)
        cosine = jnp.cos(angle_set)
        sine_part = jnp.sin(angle_set)
        lower_new = (signal + rotate(partner, cosine, sine_part)) * 0.5
        upper_new = (partner - rotate(signal, cosine, sine_part)) * 0.5
        signal = jnp.where(is_upper, upper_new, lower_new)
    return signal


def shards(raw_re, raw_im, ref_blocks, owners, offsets, taps):
    rg_cols = raw_re.shape[0]
    az_rows = raw_re.shape[1]
    az_count = lax.axis_size("az")
    az_place = lax.axis_index("az")
    bit_count = az_count.bit_length() - 1
    az_total = az_rows * az_count
    rg_total = rg_cols * lax.axis_size("rg")
    own_block = ref_blocks[0]
    lower_ref = from_root(own_block, "az", owners[0])
    upper_ref = from_root(own_block, "az", owners[1])
    signal = jnp.stack([raw_re, raw_im])
    signal = butterfly_down(signal, az_place, bit_count)
    column = jnp.zeros((), jnp.int32)
    for bit_num in range(bit_count):
        column = column + ((az_place >> bit_num & 1) << bit_count - 1 - bit_num)
    row_index = jnp.arange(az_rows, dtype=jnp.int32)
    twist = angles(row_index * column % az_total, az_total, -1.0)
    signal = rotate(signal, jnp.cos(twist)[None, :], jnp.sin(twist)[None, :])
    signal = local_dft(signal, -1.0)
    frequency = column + az_count * row_index
    signed = (frequency + az_total // 2) % az_total - az_total // 2
    az_freq = signed.astype(jnp.float32) / az_total
    rg_index = lax.axis_index("rg") * rg_cols + jnp.arange(rg_cols, dtype=jnp.int32)
    rg_freq = (rg_index.astype(jnp.float32) + 0.5) / (2 * rg_total) - 0.25
    model_phase = PHASE_GAIN * jnp.sqrt((1.0 + rg_freq)[:, None] ** 2 - az_freq[None, :] ** 2)
    ref_rows = own_block.shape[0]
    coarse = frequency * ref_rows // az_total
    slot_index = jnp.where(signed >= 0, ref_rows + coarse, coarse)
    one_hot = (jnp.arange(2 * ref_rows, dtype=jnp.int32)[:, None] == slot_index[None, :]).astype(
        jnp.float32
    )
    both_refs = jnp.concatenate([lower_ref, upper_ref], axis=0)
    picked = jnp.dot(both_refs.T, one_hot, precision=PRECISE)
    phase_all = model_phase + picked
    signal = rotate(signal, jnp.cos(phase_all), jnp.sin(phase_all))
    rim_width = REACH + TAPS // 2
    padded = padded_2(signal, (("rg", 1),), rim_width)
    offset_cols = jnp.repeat(offsets, BLOCK)
    local_cols = jnp.arange(rg_cols, dtype=jnp.int32)
    tap_index = jnp.arange(TAPS, dtype=jnp.int32)
    target = local_cols[:, None] + rim_width + offset_cols[:, None] + tap_index[None, :] - TAPS // 2
    padded_index = jnp.arange(rg_cols + 2 * rim_width, dtype=jnp.int32)
    hits = (padded_index[:, None, None] == target[None, :, :]).astype(jnp.float32)
    band_matrix = jnp.sum(hits * taps[None, :, :], axis=2)
    signal = jnp.einsum("zma,mi->zia", padded, band_matrix, precision=PRECISE)
    signal = local_dft(signal, 1.0) / az_rows
    twist_back = angles(row_index * column % az_total, az_total, 1.0)
    signal = rotate(signal, jnp.cos(twist_back)[None, :], jnp.sin(twist_back)[None, :])
    signal = butterfly_up(signal, az_place, bit_count)
    return (signal[0], signal[1])


LANES = 128
MESH = pl.DeviceIdType.MESH
RIM = REACH + TAPS // 2
TWO_PI_HI = 6.28125
TWO_PI_LO = 2.0 * math.pi - TWO_PI_HI


def split_np(matrix):
    high = matrix.astype(np.float32).astype(ml_dtypes.bfloat16)
    low = (matrix - high.astype(np.float64)).astype(np.float32).astype(ml_dtypes.bfloat16)
    return np.stack([high, low])


def tables(az_count):
    inner = LANES // az_count
    grid = np.arange(LANES)
    angle = 2.0 * np.pi * (np.outer(grid, grid) % LANES) / LANES
    cos, sin = np.cos(angle), -np.sin(angle)
    forward = [[cos, -sin], [sin, cos]]
    inverse = [[cos, sin], [-sin, cos]]
    order = np.arange(2 * LANES).reshape(2, az_count, inner).transpose(1, 0, 2).reshape(-1)
    left_in = np.block(forward)[:, order]
    right_in = np.block([[forward[o][c].T for o in range(2)] for c in range(2)])
    right_out = np.block([[inverse[o][c].T for o in range(2)] for c in range(2)])
    left_out = np.block(inverse)[order, :] / (LANES * LANES)
    matrices = np.stack([split_np(m) for m in (left_in, right_in, right_out, left_out)])
    turn = 2.0 * np.pi * np.outer(grid, grid) / (LANES * LANES)
    twiddle = np.stack([np.cos(turn), -np.sin(turn)]).astype(np.float32)
    return matrices, twiddle


def split(value):
    high = value.astype(jnp.bfloat16)
    low = (value - high.astype(jnp.float32)).astype(jnp.bfloat16)
    return high, low


def dot(a, b):
    return jnp.dot(a, b, preferred_element_type=jnp.float32)


def left_apply(table, value):
    high, low = split(value)
    return dot(table[0], high) + (dot(table[0], low) + dot(table[1], high))


def right_apply(value, table):
    high, low = split(value)
    return dot(high, table[0]) + (dot(low, table[0]) + dot(high, table[1]))


def cos_sin(phase):
    turns = jnp.floor(phase * (0.5 / math.pi) + 0.5)
    rest = (phase - turns * TWO_PI_HI) - turns * TWO_PI_LO
    half = rest * 0.5
    square = half * half
    sine = jnp.full_like(square, -1.0 / math.factorial(11))
    for power in (9, 7, 5, 3, 1):
        sine = sine * square + (-1.0) ** (power // 2) / math.factorial(power)
    sine = sine * half
    cosine = jnp.full_like(square, 1.0 / math.factorial(12))
    for power in (10, 8, 6, 4, 2, 0):
        cosine = cosine * square + (-1.0) ** (power // 2) / math.factorial(power)
    return 1.0 - 2.0 * sine * sine, 2.0 * sine * cosine


def focus_kernel(
    az_count,
    depth,
    re_hbm,
    im_hbm,
    refs_hbm,
    owners,
    matrices_hbm,
    twiddle_hbm,
    band,
    raw,
    refs,
    matrices,
    twiddle,
    outgoing,
    incoming,
    ref_out,
    ref_in,
    filt,
    focused,
    blank,
    raw_sem,
    const_sem,
    own_sem,
    ref_send,
    ref_recv,
    in_send,
    in_recv,
    back_send,
    back_recv,
    rim_send,
    rim_recv,
):
    rows = re_hbm.shape[0]
    inner = re_hbm.shape[1] // LANES
    piece = 2 * inner
    steps = rows // az_count
    me = lax.axis_index("az")
    core = lax.axis_index("rg")
    peers = []
    for flips in sorted(range(1, az_count), reverse=True):
        peer = me
        for bit in (1 << b for b in range(az_count.bit_length())):
            if flips & bit:
                peer = peer + bit - 2 * bit * lax.rem(lax.div(peer, bit), 2)
        peers.append(peer)
    sources = peers
    sibling = 1 - core
    groups = [s + (1 - core) * (steps - 1 - 2 * s) for s in range(steps)]

    def raw_copy(step, comp):
        group = pl.ds(pl.multiple_of(groups[step] * az_count, az_count), az_count)
        hbm = (re_hbm, im_hbm)[comp]
        return pltpu.make_async_copy(hbm.at[group, :], raw.at[comp, step], raw_sem.at[step, comp])

    load_refs = pltpu.make_async_copy(refs_hbm, refs, const_sem.at[2])
    load_refs.start()
    for step in range(steps):
        for comp in range(2):
            raw_copy(step, comp).start()

    barrier = pltpu.get_barrier_semaphore()
    for peer in peers:
        pl.semaphore_signal(barrier, inc=1, device_id={"az": peer}, device_id_type=MESH)
    pl.semaphore_signal(barrier, inc=1, device_id={"rg": sibling}, device_id_type=MESH)
    load_matrices = pltpu.make_async_copy(matrices_hbm, matrices, const_sem.at[0])
    load_twiddle = pltpu.make_async_copy(twiddle_hbm, twiddle, const_sem.at[1])
    load_matrices.start()
    load_twiddle.start()

    def at(start, count):
        return pl.ds(start * piece if isinstance(start, int) else pl.multiple_of(start * piece, piece), count * piece)

    ref_rows = refs.shape[1]
    coarse = lax.broadcasted_iota(jnp.int32, (ref_rows, LANES), 0)
    column = lax.broadcasted_iota(jnp.int32, (ref_rows, LANES), 1)
    spread = (coarse == column // (LANES // ref_rows)).astype(jnp.float32)
    load_refs.wait()
    wide = jnp.dot(refs[...], spread, precision=PRECISE, preferred_element_type=jnp.float32)
    ref_out[...] = jnp.zeros_like(ref_out)
    for dest in range(az_count):
        for group in range(steps):
            row = group * az_count + dest
            ref_out[dest, group : group + 1, :] = wide[row : row + 1, :]

    def ref_copy(s, peer, source):
        return pltpu.make_async_remote_copy(
            src_ref=ref_out.at[peer],
            dst_ref=ref_in.at[source],
            send_sem=ref_send.at[s],
            recv_sem=ref_recv.at[source],
            device_id={"az": peer},
            device_id_type=MESH,
        )

    def in_copy(step, s, peer, source):
        return pltpu.make_async_remote_copy(
            src_ref=outgoing.at[at(groups[step] * az_count + peer, 1), :],
            dst_ref=incoming.at[at(groups[step] * az_count + source, 1), :],
            send_sem=in_send.at[step, s],
            recv_sem=in_recv.at[step, source],
            device_id={"az": peer},
            device_id_type=MESH,
        )

    def back_copy(step, s, peer, source):
        return pltpu.make_async_remote_copy(
            src_ref=focused.at[at(groups[step] * az_count + peer, 1), :],
            dst_ref=band.at[at(RIM + groups[step] * az_count + source, 1), :],
            send_sem=back_send.at[step, s],
            recv_sem=back_recv.at[step, source],
            device_id={"az": peer},
            device_id_type=MESH,
        )

    def own_copy(step):
        row = groups[step] * az_count + me
        return pltpu.make_async_copy(focused.at[at(row, 1), :], band.at[at(RIM + row, 1), :], own_sem.at[step])

    def rim_copy(step):
        count = (az_count, RIM - az_count)[step]
        first = ((rows - az_count, rows - RIM)[step], (0, az_count)[step])
        place = ((RIM - az_count, 0)[step], (RIM + rows, RIM + rows + az_count)[step])
        return pltpu.make_async_remote_copy(
            src_ref=band.at[at(RIM + first[0] * (1 - core) + first[1] * core, count), :],
            dst_ref=band.at[at(place[0] * (1 - core) + place[1] * core, count), :],
            send_sem=rim_send.at[step],
            recv_sem=rim_recv.at[step],
            device_id={"rg": sibling},
            device_id_type=MESH,
        )

    def rim_arrival(step):
        count = (az_count, RIM - az_count)[step]
        place = ((RIM - az_count, 0)[step], (RIM + rows, RIM + rows + az_count)[step])
        return pltpu.make_async_remote_copy(
            src_ref=band.at[at(RIM, count), :],
            dst_ref=band.at[at(place[0] * core + place[1] * (1 - core), count), :],
            send_sem=rim_send.at[step],
            recv_sem=rim_recv.at[step],
            device_id={"rg": sibling},
            device_id_type=MESH,
        )

    for step in range(steps):
        for comp in range(2):
            raw_copy(step, comp).wait()
            for i in range(inner):
                place = groups[step] * (az_count * piece) + (comp * inner + i)
                outgoing[pl.ds(place, az_count, stride=piece), :] = raw[comp, step, :, i * LANES : (i + 1) * LANES]
        if step == 0:
            pl.semaphore_wait(barrier, az_count)
            for s, peer in enumerate(peers):
                ref_copy(s, peer, me).start()
        for s, peer in enumerate(peers):
            in_copy(step, s, peer, me).start()
        own = at(groups[step] * az_count + me, 1)
        incoming[own, :] = outgoing[own, :]

    ref_in[me] = ref_out[me]
    blank[...] = jnp.zeros_like(blank)
    spare = depth - rows - 2 * RIM
    clear_rim = pltpu.make_async_copy(blank, band.at[at((RIM + rows) * core, RIM), :], const_sem.at[3])
    clear_rim.start()
    clear_spare = pltpu.make_async_copy(
        blank.at[at(0, spare), :], band.at[at(depth - spare, spare), :], const_sem.at[4]
    )
    clear_spare.start()

    for s, source in enumerate(sources):
        ref_copy(s, peers[s], source).wait_recv()
    lane = lax.broadcasted_iota(jnp.int32, ref_in.shape[1:], 1)
    picked = jnp.zeros(ref_in.shape[1:], jnp.float32)
    for source in range(az_count):
        wanted = jnp.where(lane < LANES // 2, owners[1], owners[0]) == source
        picked = jnp.where(wanted, ref_in[source], picked)
    az_total = LANES * LANES
    low = lax.broadcasted_iota(jnp.int32, (LANES, LANES), 0)
    high = lax.broadcasted_iota(jnp.int32, (LANES, LANES), 1)
    frequency = low + LANES * high
    signed = jnp.where(frequency >= az_total // 2, frequency - az_total, frequency)
    az_freq = signed.astype(jnp.float32) / az_total
    az_square = az_freq * az_freq
    for group in range(steps):
        index = core * rows + group * az_count + me
        rg_freq = 1.0 + ((index.astype(jnp.float32) + 0.5) * (1.0 / (4 * rows)) - 0.25)
        phase = PHASE_GAIN * jnp.sqrt(rg_freq * rg_freq - az_square) + picked[group : group + 1, :]
        cosine, sine = cos_sin(phase)
        filt[group, 0] = cosine
        filt[group, 1] = sine

    load_matrices.wait()
    load_twiddle.wait()
    for step in range(steps):
        group = groups[step]
        for s, source in enumerate(sources):
            in_copy(step, s, peers[s], source).wait_recv()
        whole = at(group * az_count, az_count)
        value = left_apply((matrices[0, 0], matrices[0, 1]), incoming[whole, :])
        cosine, sine = twiddle[0], twiddle[1]
        real, imag = value[:LANES], value[LANES:]
        value = jnp.concatenate([real * cosine - imag * sine, real * sine + imag * cosine], axis=1)
        value = right_apply(value, (matrices[1, 0], matrices[1, 1]))
        real, imag = value[:, :LANES], value[:, LANES:]
        cosine, sine = filt[group, 0], filt[group, 1]
        value = jnp.concatenate([real * cosine - imag * sine, real * sine + imag * cosine], axis=1)
        value = right_apply(value, (matrices[2, 0], matrices[2, 1]))
        real, imag = value[:, :LANES], value[:, LANES:]
        cosine, sine = twiddle[0], twiddle[1]
        value = jnp.concatenate([real * cosine + imag * sine, imag * cosine - real * sine], axis=0)
        focused[whole, :] = left_apply((matrices[3, 0], matrices[3, 1]), value)
        for s, peer in enumerate(peers):
            back_copy(step, s, peer, me).start()
        own_copy(step).start()
        if step >= steps - 2:
            early = step - (steps - 2)
            for s, source in enumerate(sources):
                back_copy(early, s, peers[s], source).wait_recv()
            own_copy(early).wait()
            rim_copy(early).start()
    clear_rim.wait()
    clear_spare.wait()
    for step in range(2, steps):
        own_copy(step).wait()
        for s, source in enumerate(sources):
            back_copy(step, s, peers[s], source).wait_recv()
    for step in range(2):
        rim_arrival(step).wait_recv()

    for s, peer in enumerate(peers):
        ref_copy(s, peer, me).wait_send()
        for step in range(steps):
            in_copy(step, s, peer, me).wait_send()
            back_copy(step, s, peer, me).wait_send()
    for step in range(2):
        rim_copy(step).wait_send()


def stolt_kernel(piece, band_hbm, offsets, taps, out_re, out_im, band, image, in_sem, out_sem):
    depth = band.shape[0] // piece
    inner = piece // 2
    half = inner // 2
    rows = out_re.shape[0]
    outs = (out_re, out_im)
    loads = in_sem.shape[0]

    def load(part):
        lines = pl.ds(part * (band.shape[0] // loads), band.shape[0] // loads)
        return pltpu.make_async_copy(band_hbm.at[lines, :], band.at[lines, :], in_sem.at[part])

    def save(comp, part):
        columns = pl.ds(part * half * LANES, half * LANES)
        return pltpu.make_async_copy(image.at[comp, :, columns], outs[comp].at[:, columns], out_sem.at[comp, part])

    for part in range(loads):
        load(part).start()
    slot = lax.broadcasted_iota(jnp.int32, (depth, rows), 0)
    target = lax.broadcasted_iota(jnp.int32, (depth, rows), 1)
    target_block = target // BLOCK
    for block in range(rows // BLOCK):
        target = jnp.where(target_block == block, target + offsets[block], target)
    weights = jnp.zeros((depth, rows), jnp.float32)
    for tap in range(TAPS):
        weights = weights + jnp.where(slot == target + (RIM + tap - TAPS // 2), taps[tap : tap + 1, :], 0.0)
    high, low = split(weights.T)
    weights = jnp.concatenate([high, high, low], axis=1)
    for part in range(loads):
        load(part).wait()
    for comp in range(2):
        for part in range(2):
            for i in range(part * half, part * half + half, 2):
                value = jnp.concatenate(
                    [band[pl.ds(comp * inner + i + j, depth, stride=piece), :] for j in range(2)], axis=1
                )
                high, low = split(value)
                value = dot(weights, jnp.concatenate([high, low, high], axis=0))
                image[comp, :, i * LANES : (i + 2) * LANES] = value
            save(comp, part).start()
    for comp in range(2):
        for part in range(2):
            save(comp, part).wait()


def fused_shards(az_count, raw_re, raw_im, ref_blocks, owners, offsets, taps):
    rows, samples = raw_re.shape
    ref_rows = ref_blocks.shape[1]
    piece = 2 * samples // LANES
    steps = rows // az_count
    depth = -(-(rows + 2 * RIM) // 16) * 16
    matrices, twiddle = tables(az_count)
    smem = pl.BlockSpec(memory_space=pltpu.SMEM)
    hbm = pl.BlockSpec(memory_space=pl.ANY)
    dma = pltpu.SemaphoreType.DMA
    flat = pltpu.VMEM((rows * piece, LANES), jnp.float32)
    band = pl.pallas_call(
        functools.partial(focus_kernel, az_count, depth),
        out_shape=jax.ShapeDtypeStruct((depth * piece, LANES), jnp.float32),
        in_specs=[hbm, hbm, hbm, smem, hbm, hbm],
        out_specs=hbm,
        scratch_shapes=[
            pltpu.VMEM((2, steps, az_count, samples), jnp.float32),
            pltpu.VMEM((rows, ref_rows), jnp.float32),
            pltpu.VMEM(matrices.shape, jnp.bfloat16),
            pltpu.VMEM(twiddle.shape, jnp.float32),
            flat,
            flat,
            pltpu.VMEM((az_count, 8, LANES), jnp.float32),
            pltpu.VMEM((az_count, 8, LANES), jnp.float32),
            pltpu.VMEM((steps, 2, LANES, LANES), jnp.float32),
            flat,
            pltpu.VMEM((RIM * piece, LANES), jnp.float32),
            dma((steps, 2)),
            dma((5,)),
            dma((steps,)),
            dma((az_count,)),
            dma((az_count,)),
            dma((steps, az_count)),
            dma((steps, az_count)),
            dma((steps, az_count)),
            dma((steps, az_count)),
            dma((2,)),
            dma((2,)),
        ],
        compiler_params=pltpu.CompilerParams(
            collective_id=0, has_side_effects=True, vmem_limit_bytes=62 * 1024 * 1024
        ),
    )(raw_re, raw_im, ref_blocks[0].T, owners, jnp.asarray(matrices), jnp.asarray(twiddle))
    vmem = pl.BlockSpec(memory_space=pltpu.VMEM)
    return pl.pallas_call(
        functools.partial(stolt_kernel, piece),
        out_shape=[jax.ShapeDtypeStruct(raw_re.shape, jnp.float32)] * 2,
        in_specs=[hbm, smem, vmem],
        out_specs=[hbm, hbm],
        scratch_shapes=[
            pltpu.VMEM((depth * piece, LANES), jnp.float32),
            pltpu.VMEM((2, rows, samples), jnp.float32),
            dma((4,)),
            dma((2, 2)),
        ],
        compiler_params=pltpu.CompilerParams(vmem_limit_bytes=62 * 1024 * 1024),
    )(band, offsets, taps.T)


def body_for(mesh):
    az_count, rg_count = mesh.shape["az"], mesh.shape["rg"]

    def body(raw_re, raw_im, ref_blocks, owners, offsets, taps):
        rows, samples = raw_re.shape
        fits = (
            samples * az_count == LANES * LANES
            and az_count == 8
            and rows == 4 * az_count
            and rg_count == 2
            and ref_blocks.shape[1] == 64
        )
        if fits:
            return tuple(fused_shards(az_count, raw_re, raw_im, ref_blocks, owners, offsets, taps))
        return shards(raw_re, raw_im, ref_blocks, owners, offsets, taps)

    return body


def solution(mesh):
    return jax.shard_map(
        body_for(mesh),
        mesh=mesh,
        in_specs=(
            P("rg", ("scene", "az")),
            P("rg", ("scene", "az")),
            P(("scene", "az"), None, "rg"),
            P("scene"),
            P("rg"),
            P("rg", None),
        ),
        out_specs=(P("rg", ("scene", "az")), P("rg", ("scene", "az"))),
        check_vma=False,
    )
```

```python
import functools
import math

import jax
import jax.numpy as jnp
import ml_dtypes
import numpy as np
from jax import lax
from jax.experimental import pallas as pl
from jax.experimental.pallas import tpu as pltpu
from jax.sharding import PartitionSpec as P

SPLIT = 4
TAPS = 8
REACH = 8
BLOCK = 16


PRECISE = lax.Precision.HIGHEST
PHASE_GAIN = 50.0


def partner_2(value, axis, stride):
    return lax.ppermute(value, axis, [(i, i ^ 1 << stride) for i in range(lax.axis_size(axis))])


def from_root(block, axis, source):
    block = jnp.where(lax.axis_index(axis) == source, block, jnp.zeros_like(block))
    return lax.psum(block, axis)


def padded_2(value, sides, width):
    for axis, dim in sides:
        size, length = (lax.axis_size(axis), value.shape[dim])
        up = [(i, (i + 1) % size) for i in range(size - 1)]
        down = [(j, i) for i, j in up]
        last = lax.slice_in_dim(value, length - width, length, axis=dim)
        initial = lax.slice_in_dim(value, 0, width, axis=dim)
        before = lax.ppermute(last, axis, up)
        after = lax.ppermute(initial, axis, down)
        value = jnp.concatenate([before, value, after], axis=dim)
    return value


def angles(numerator, denominator, sign_value):
    return sign_value * 2.0 * math.pi * numerator.astype(jnp.float32) / denominator


def rotate(signal, cosine, sine_part):
    real_part = signal[0] * cosine - signal[1] * sine_part
    imag_part = signal[0] * sine_part + signal[1] * cosine
    return jnp.stack([real_part, imag_part])


def dft_table(length_n, sign_value):
    counter = jnp.arange(length_n, dtype=jnp.int32)
    turn_count = counter[:, None] * counter[None, :] % length_n
    angle_set = angles(turn_count, length_n, sign_value)
    return (jnp.cos(angle_set), jnp.sin(angle_set))


def complex_apply(einsum_form, cosine, sine_part, signal):
    real_part = jnp.einsum(einsum_form, cosine, signal[0], precision=PRECISE) - jnp.einsum(
        einsum_form, sine_part, signal[1], precision=PRECISE
    )
    imag_part = jnp.einsum(einsum_form, cosine, signal[1], precision=PRECISE) + jnp.einsum(
        einsum_form, sine_part, signal[0], precision=PRECISE
    )
    return jnp.stack([real_part, imag_part])


def local_dft(signal, sign_value):
    rg_cols = signal.shape[1]
    az_rows = signal.shape[2]
    inner_len = az_rows // SPLIT
    shaped = signal.reshape(2, rg_cols, SPLIT, inner_len)
    first_cos, first_sin = dft_table(SPLIT, sign_value)
    first_pass = complex_apply("aj,cjk->cak", first_cos, first_sin, shaped)
    outer_idx = jnp.arange(SPLIT, dtype=jnp.int32)
    inner_idx = jnp.arange(inner_len, dtype=jnp.int32)
    twist = angles(outer_idx[:, None] * inner_idx[None, :] % az_rows, az_rows, sign_value)
    first_pass = rotate(first_pass, jnp.cos(twist)[None, :, :], jnp.sin(twist)[None, :, :])
    second_cos, second_sin = dft_table(inner_len, sign_value)
    second_pass = complex_apply("bk,cak->cba", second_cos, second_sin, first_pass)
    return second_pass.reshape(2, rg_cols, az_rows)


def butterfly_down(signal, az_place, bit_count):
    for bit_num in reversed(range(bit_count)):
        half_span = 1 << bit_num
        partner = partner_2(signal, "az", bit_num)
        is_upper = az_place >> bit_num & 1 == 1
        angle_set = angles(az_place % half_span, 2 * half_span, -1.0)
        difference = rotate(partner - signal, jnp.cos(angle_set), jnp.sin(angle_set))
        signal = jnp.where(is_upper, difference, signal + partner)
    return signal


def butterfly_up(signal, az_place, bit_count):
    for bit_num in range(bit_count):
        half_span = 1 << bit_num
        partner = partner_2(signal, "az", bit_num)
        is_upper = az_place >> bit_num & 1 == 1
        angle_set = angles(az_place % half_span, 2 * half_span, 1.0)
        cosine = jnp.cos(angle_set)
        sine_part = jnp.sin(angle_set)
        lower_new = (signal + rotate(partner, cosine, sine_part)) * 0.5
        upper_new = (partner - rotate(signal, cosine, sine_part)) * 0.5
        signal = jnp.where(is_upper, upper_new, lower_new)
    return signal


def shards(raw_re, raw_im, ref_blocks, owners, offsets, taps):
    rg_cols = raw_re.shape[0]
    az_rows = raw_re.shape[1]
    az_count = lax.axis_size("az")
    az_place = lax.axis_index("az")
    bit_count = az_count.bit_length() - 1
    az_total = az_rows * az_count
    rg_total = rg_cols * lax.axis_size("rg")
    own_block = ref_blocks[0]
    lower_ref = from_root(own_block, "az", owners[0])
    upper_ref = from_root(own_block, "az", owners[1])
    signal = jnp.stack([raw_re, raw_im])
    signal = butterfly_down(signal, az_place, bit_count)
    column = jnp.zeros((), jnp.int32)
    for bit_num in range(bit_count):
        column = column + ((az_place >> bit_num & 1) << bit_count - 1 - bit_num)
    row_index = jnp.arange(az_rows, dtype=jnp.int32)
    twist = angles(row_index * column % az_total, az_total, -1.0)
    signal = rotate(signal, jnp.cos(twist)[None, :], jnp.sin(twist)[None, :])
    signal = local_dft(signal, -1.0)
    frequency = column + az_count * row_index
    signed = (frequency + az_total // 2) % az_total - az_total // 2
    az_freq = signed.astype(jnp.float32) / az_total
    rg_index = lax.axis_index("rg") * rg_cols + jnp.arange(rg_cols, dtype=jnp.int32)
    rg_freq = (rg_index.astype(jnp.float32) + 0.5) / (2 * rg_total) - 0.25
    model_phase = PHASE_GAIN * jnp.sqrt((1.0 + rg_freq)[:, None] ** 2 - az_freq[None, :] ** 2)
    ref_rows = own_block.shape[0]
    coarse = frequency * ref_rows // az_total
    slot_index = jnp.where(signed >= 0, ref_rows + coarse, coarse)
    one_hot = (jnp.arange(2 * ref_rows, dtype=jnp.int32)[:, None] == slot_index[None, :]).astype(
        jnp.float32
    )
    both_refs = jnp.concatenate([lower_ref, upper_ref], axis=0)
    picked = jnp.dot(both_refs.T, one_hot, precision=PRECISE)
    phase_all = model_phase + picked
    signal = rotate(signal, jnp.cos(phase_all), jnp.sin(phase_all))
    rim_width = REACH + TAPS // 2
    padded = padded_2(signal, (("rg", 1),), rim_width)
    offset_cols = jnp.repeat(offsets, BLOCK)
    local_cols = jnp.arange(rg_cols, dtype=jnp.int32)
    tap_index = jnp.arange(TAPS, dtype=jnp.int32)
    target = local_cols[:, None] + rim_width + offset_cols[:, None] + tap_index[None, :] - TAPS // 2
    padded_index = jnp.arange(rg_cols + 2 * rim_width, dtype=jnp.int32)
    hits = (padded_index[:, None, None] == target[None, :, :]).astype(jnp.float32)
    band_matrix = jnp.sum(hits * taps[None, :, :], axis=2)
    signal = jnp.einsum("zma,mi->zia", padded, band_matrix, precision=PRECISE)
    signal = local_dft(signal, 1.0) / az_rows
    twist_back = angles(row_index * column % az_total, az_total, 1.0)
    signal = rotate(signal, jnp.cos(twist_back)[None, :], jnp.sin(twist_back)[None, :])
    signal = butterfly_up(signal, az_place, bit_count)
    return (signal[0], signal[1])


LANES = 128
MESH = pl.DeviceIdType.MESH
RIM = REACH + TAPS // 2
TWO_PI_HI = 6.28125
TWO_PI_LO = 2.0 * math.pi - TWO_PI_HI


def split_np(matrix):
    high = matrix.astype(np.float32).astype(ml_dtypes.bfloat16)
    low = (matrix - high.astype(np.float64)).astype(np.float32).astype(ml_dtypes.bfloat16)
    return np.stack([high, low])


def tables(az_count):
    inner = LANES // az_count
    grid = np.arange(LANES)
    angle = 2.0 * np.pi * (np.outer(grid, grid) % LANES) / LANES
    cos, sin = np.cos(angle), -np.sin(angle)
    forward = [[cos, -sin], [sin, cos]]
    inverse = [[cos, sin], [-sin, cos]]
    order = np.arange(2 * LANES).reshape(2, az_count, inner).transpose(1, 0, 2).reshape(-1)
    left_in = np.block(forward)[:, order]
    right_in = np.block([[forward[o][c].T for o in range(2)] for c in range(2)])
    right_out = np.block([[inverse[o][c].T for o in range(2)] for c in range(2)])
    left_out = np.block(inverse)[order, :] / (LANES * LANES)
    matrices = np.stack([split_np(m) for m in (left_in, right_in, right_out, left_out)])
    turn = 2.0 * np.pi * np.outer(grid, grid) / (LANES * LANES)
    twiddle = np.stack([np.cos(turn), -np.sin(turn)]).astype(np.float32)
    return matrices, twiddle


def split(value):
    high = value.astype(jnp.bfloat16)
    low = (value - high.astype(jnp.float32)).astype(jnp.bfloat16)
    return high, low


def dot(a, b):
    return jnp.dot(a, b, preferred_element_type=jnp.float32)


def left_apply(table, value):
    high, low = split(value)
    return dot(table[0], high) + (dot(table[0], low) + dot(table[1], high))


def right_apply(value, table):
    high, low = split(value)
    return dot(high, table[0]) + (dot(low, table[0]) + dot(high, table[1]))


def cos_sin(phase):
    turns = jnp.floor(phase * (0.5 / math.pi) + 0.5)
    rest = (phase - turns * TWO_PI_HI) - turns * TWO_PI_LO
    half = rest * 0.5
    square = half * half
    sine = jnp.full_like(square, -1.0 / math.factorial(11))
    for power in (9, 7, 5, 3, 1):
        sine = sine * square + (-1.0) ** (power // 2) / math.factorial(power)
    sine = sine * half
    cosine = jnp.full_like(square, 1.0 / math.factorial(12))
    for power in (10, 8, 6, 4, 2, 0):
        cosine = cosine * square + (-1.0) ** (power // 2) / math.factorial(power)
    return 1.0 - 2.0 * sine * sine, 2.0 * sine * cosine


def focus_kernel(
    az_count,
    depth,
    re_hbm,
    im_hbm,
    refs_hbm,
    owners,
    matrices_hbm,
    twiddle_hbm,
    band,
    raw,
    refs,
    matrices,
    twiddle,
    outgoing,
    incoming,
    ref_out,
    ref_in,
    filt,
    focused,
    blank,
    chosen,
    raw_sem,
    const_sem,
    own_sem,
    ref_send,
    ref_recv,
    in_send,
    in_recv,
    back_send,
    back_recv,
    rim_send,
    rim_recv,
):
    rows = re_hbm.shape[0]
    inner = re_hbm.shape[1] // LANES
    piece = 2 * inner
    steps = rows // az_count
    me = lax.axis_index("az")
    core = lax.axis_index("rg")
    peers = []
    for flips in sorted(range(1, az_count), reverse=True):
        peer = me
        for bit in (1 << b for b in range(az_count.bit_length())):
            if flips & bit:
                peer = peer + bit - 2 * bit * lax.rem(lax.div(peer, bit), 2)
        peers.append(peer)
    sources = peers
    sibling = 1 - core
    def group_of(step):
        return step + (1 - core) * (steps - 1 - 2 * step)

    def each(count, action):
        def run(index, carry):
            action(index)
            return carry

        lax.fori_loop(0, count, run, 0)

    def raw_copy(step, comp):
        group = pl.ds(pl.multiple_of(group_of(step) * az_count, az_count), az_count)
        hbm = (re_hbm, im_hbm)[comp]
        return pltpu.make_async_copy(hbm.at[group, :], raw.at[comp, step], raw_sem.at[step, comp])

    load_refs = pltpu.make_async_copy(refs_hbm, refs, const_sem.at[2])
    load_refs.start()
    for step in range(steps):
        for comp in range(2):
            raw_copy(step, comp).start()

    barrier = pltpu.get_barrier_semaphore()
    for peer in peers:
        pl.semaphore_signal(barrier, inc=1, device_id={"az": peer}, device_id_type=MESH)
    pl.semaphore_signal(barrier, inc=1, device_id={"rg": sibling}, device_id_type=MESH)
    load_matrices = pltpu.make_async_copy(matrices_hbm, matrices, const_sem.at[0])
    load_twiddle = pltpu.make_async_copy(twiddle_hbm, twiddle, const_sem.at[1])
    load_matrices.start()
    load_twiddle.start()

    def at(start, count):
        return pl.ds(start * piece if isinstance(start, int) else pl.multiple_of(start * piece, piece), count * piece)

    ref_rows = refs.shape[1]
    coarse = lax.broadcasted_iota(jnp.int32, (ref_rows, LANES), 0)
    column = lax.broadcasted_iota(jnp.int32, (ref_rows, LANES), 1)
    spread = (coarse == column // (LANES // ref_rows)).astype(jnp.float32)
    load_refs.wait()
    wide = jnp.dot(refs[...], spread, precision=PRECISE, preferred_element_type=jnp.float32)
    ref_out[...] = jnp.zeros_like(ref_out)
    for dest in range(az_count):
        for group in range(steps):
            row = group * az_count + dest
            ref_out[dest, group : group + 1, :] = wide[row : row + 1, :]

    def ref_copy(s, peer, source):
        return pltpu.make_async_remote_copy(
            src_ref=ref_out.at[peer],
            dst_ref=ref_in.at[source],
            send_sem=ref_send.at[s],
            recv_sem=ref_recv.at[source],
            device_id={"az": peer},
            device_id_type=MESH,
        )

    def in_copy(step, s, peer, source):
        return pltpu.make_async_remote_copy(
            src_ref=outgoing.at[at(group_of(step) * az_count + peer, 1), :],
            dst_ref=incoming.at[at(group_of(step) * az_count + source, 1), :],
            send_sem=in_send.at[step, s],
            recv_sem=in_recv.at[step, source],
            device_id={"az": peer},
            device_id_type=MESH,
        )

    def back_copy(step, s, peer, source):
        return pltpu.make_async_remote_copy(
            src_ref=focused.at[at(group_of(step) * az_count + peer, 1), :],
            dst_ref=band.at[at(RIM + group_of(step) * az_count + source, 1), :],
            send_sem=back_send.at[step, s],
            recv_sem=back_recv.at[step, source],
            device_id={"az": peer},
            device_id_type=MESH,
        )

    def own_copy(step):
        row = group_of(step) * az_count + me
        return pltpu.make_async_copy(focused.at[at(row, 1), :], band.at[at(RIM + row, 1), :], own_sem.at[step])

    def rim_copy(step):
        count = (az_count, RIM - az_count)[step]
        first = ((rows - az_count, rows - RIM)[step], (0, az_count)[step])
        place = ((RIM - az_count, 0)[step], (RIM + rows, RIM + rows + az_count)[step])
        return pltpu.make_async_remote_copy(
            src_ref=band.at[at(RIM + first[0] * (1 - core) + first[1] * core, count), :],
            dst_ref=band.at[at(place[0] * (1 - core) + place[1] * core, count), :],
            send_sem=rim_send.at[step],
            recv_sem=rim_recv.at[step],
            device_id={"rg": sibling},
            device_id_type=MESH,
        )

    def rim_arrival(step):
        count = (az_count, RIM - az_count)[step]
        place = ((RIM - az_count, 0)[step], (RIM + rows, RIM + rows + az_count)[step])
        return pltpu.make_async_remote_copy(
            src_ref=band.at[at(RIM, count), :],
            dst_ref=band.at[at(place[0] * core + place[1] * (1 - core), count), :],
            send_sem=rim_send.at[step],
            recv_sem=rim_recv.at[step],
            device_id={"rg": sibling},
            device_id_type=MESH,
        )

    pl.semaphore_wait(barrier, az_count)
    for s, peer in enumerate(peers):
        ref_copy(s, peer, me).start()

    def send(step):
        for comp in range(2):
            raw_copy(step, comp).wait()
            for i in range(inner):
                place = group_of(step) * (az_count * piece) + (comp * inner + i)
                outgoing[pl.ds(place, az_count, stride=piece), :] = raw[comp, step, :, i * LANES : (i + 1) * LANES]
        for s, peer in enumerate(peers):
            in_copy(step, s, peer, me).start()
        own = at(group_of(step) * az_count + me, 1)
        incoming[own, :] = outgoing[own, :]

    each(steps, send)

    ref_in[me] = ref_out[me]
    blank[...] = jnp.zeros_like(blank)
    spare = depth - rows - 2 * RIM
    clear_rim = pltpu.make_async_copy(blank, band.at[at((RIM + rows) * core, RIM), :], const_sem.at[3])
    clear_rim.start()
    clear_spare = pltpu.make_async_copy(
        blank.at[at(0, spare), :], band.at[at(depth - spare, spare), :], const_sem.at[4]
    )
    clear_spare.start()

    for s, source in enumerate(sources):
        ref_copy(s, peers[s], source).wait_recv()
    lane = lax.broadcasted_iota(jnp.int32, ref_in.shape[1:], 1)
    picked = jnp.zeros(ref_in.shape[1:], jnp.float32)
    for source in range(az_count):
        wanted = jnp.where(lane < LANES // 2, owners[1], owners[0]) == source
        picked = jnp.where(wanted, ref_in[source], picked)
    chosen[...] = picked
    az_total = LANES * LANES
    low = lax.broadcasted_iota(jnp.int32, (LANES, LANES), 0)
    high = lax.broadcasted_iota(jnp.int32, (LANES, LANES), 1)
    frequency = low + LANES * high
    signed = jnp.where(frequency >= az_total // 2, frequency - az_total, frequency)
    az_freq = signed.astype(jnp.float32) / az_total
    az_square = az_freq * az_freq
    def make_filter(group):
        index = core * rows + group * az_count + me
        rg_freq = 1.0 + ((index.astype(jnp.float32) + 0.5) * (1.0 / (4 * rows)) - 0.25)
        phase = PHASE_GAIN * jnp.sqrt(rg_freq * rg_freq - az_square) + chosen[pl.ds(group, 1), :]
        cosine, sine = cos_sin(phase)
        filt[group, 0] = cosine
        filt[group, 1] = sine

    each(steps, make_filter)

    load_matrices.wait()
    load_twiddle.wait()
    def arrive(step):
        own_copy(step).wait()
        for s, source in enumerate(sources):
            back_copy(step, s, peers[s], source).wait_recv()

    def focus(step):
        group = group_of(step)
        for s, source in enumerate(sources):
            in_copy(step, s, peers[s], source).wait_recv()
        whole = at(group * az_count, az_count)
        value = left_apply((matrices[0, 0], matrices[0, 1]), incoming[whole, :])
        cosine, sine = twiddle[0], twiddle[1]
        real, imag = value[:LANES], value[LANES:]
        value = jnp.concatenate([real * cosine - imag * sine, real * sine + imag * cosine], axis=1)
        value = right_apply(value, (matrices[1, 0], matrices[1, 1]))
        real, imag = value[:, :LANES], value[:, LANES:]
        cosine, sine = filt[group, 0], filt[group, 1]
        value = jnp.concatenate([real * cosine - imag * sine, real * sine + imag * cosine], axis=1)
        value = right_apply(value, (matrices[2, 0], matrices[2, 1]))
        real, imag = value[:, :LANES], value[:, LANES:]
        cosine, sine = twiddle[0], twiddle[1]
        value = jnp.concatenate([real * cosine + imag * sine, imag * cosine - real * sine], axis=0)
        focused[whole, :] = left_apply((matrices[3, 0], matrices[3, 1]), value)
        for s, peer in enumerate(peers):
            back_copy(step, s, peer, me).start()
        own_copy(step).start()

    each(steps, focus)
    for step in range(2):
        arrive(step)
        rim_copy(step).start()
    clear_rim.wait()
    clear_spare.wait()
    each(steps - 2, lambda step: arrive(step + 2))
    for step in range(2):
        rim_arrival(step).wait_recv()

    def sent(step):
        for s, peer in enumerate(peers):
            in_copy(step, s, peer, me).wait_send()
            back_copy(step, s, peer, me).wait_send()

    each(steps, sent)
    for s, peer in enumerate(peers):
        ref_copy(s, peer, me).wait_send()
    for step in range(2):
        rim_copy(step).wait_send()


def stolt_kernel(piece, band_hbm, offsets, taps, out_re, out_im, band, image, in_sem, out_sem):
    depth = band.shape[0] // piece
    inner = piece // 2
    half = inner // 2
    rows = out_re.shape[0]
    outs = (out_re, out_im)
    loads = in_sem.shape[0]

    def load(part):
        lines = pl.ds(part * (band.shape[0] // loads), band.shape[0] // loads)
        return pltpu.make_async_copy(band_hbm.at[lines, :], band.at[lines, :], in_sem.at[part])

    def save(comp, part):
        columns = pl.ds(part * half * LANES, half * LANES)
        return pltpu.make_async_copy(image.at[comp, :, columns], outs[comp].at[:, columns], out_sem.at[comp, part])

    for part in range(loads):
        load(part).start()
    slot = lax.broadcasted_iota(jnp.int32, (depth, rows), 0)
    target = lax.broadcasted_iota(jnp.int32, (depth, rows), 1)
    target_block = target // BLOCK
    for block in range(rows // BLOCK):
        target = jnp.where(target_block == block, target + offsets[block], target)
    weights = jnp.zeros((depth, rows), jnp.float32)
    for tap in range(TAPS):
        weights = weights + jnp.where(slot == target + (RIM + tap - TAPS // 2), taps[tap : tap + 1, :], 0.0)
    high, low = split(weights.T)
    weights = jnp.concatenate([high, high, low], axis=1)
    for part in range(loads):
        load(part).wait()
    for comp in range(2):
        for part in range(2):
            for i in range(part * half, part * half + half, 2):
                value = jnp.concatenate(
                    [band[pl.ds(comp * inner + i + j, depth, stride=piece), :] for j in range(2)], axis=1
                )
                high, low = split(value)
                value = dot(weights, jnp.concatenate([high, low, high], axis=0))
                image[comp, :, i * LANES : (i + 2) * LANES] = value
            save(comp, part).start()
    for comp in range(2):
        for part in range(2):
            save(comp, part).wait()


def fused_shards(az_count, raw_re, raw_im, ref_blocks, owners, offsets, taps):
    rows, samples = raw_re.shape
    ref_rows = ref_blocks.shape[1]
    piece = 2 * samples // LANES
    steps = rows // az_count
    depth = -(-(rows + 2 * RIM) // 16) * 16
    matrices, twiddle = tables(az_count)
    smem = pl.BlockSpec(memory_space=pltpu.SMEM)
    hbm = pl.BlockSpec(memory_space=pl.ANY)
    dma = pltpu.SemaphoreType.DMA
    flat = pltpu.VMEM((rows * piece, LANES), jnp.float32)
    band = pl.pallas_call(
        functools.partial(focus_kernel, az_count, depth),
        out_shape=jax.ShapeDtypeStruct((depth * piece, LANES), jnp.float32),
        in_specs=[hbm, hbm, hbm, smem, hbm, hbm],
        out_specs=hbm,
        scratch_shapes=[
            pltpu.VMEM((2, steps, az_count, samples), jnp.float32),
            pltpu.VMEM((rows, ref_rows), jnp.float32),
            pltpu.VMEM(matrices.shape, jnp.bfloat16),
            pltpu.VMEM(twiddle.shape, jnp.float32),
            flat,
            flat,
            pltpu.VMEM((az_count, 8, LANES), jnp.float32),
            pltpu.VMEM((az_count, 8, LANES), jnp.float32),
            pltpu.VMEM((steps, 2, LANES, LANES), jnp.float32),
            flat,
            pltpu.VMEM((RIM * piece, LANES), jnp.float32),
            pltpu.VMEM((8, LANES), jnp.float32),
            dma((steps, 2)),
            dma((5,)),
            dma((steps,)),
            dma((az_count,)),
            dma((az_count,)),
            dma((steps, az_count)),
            dma((steps, az_count)),
            dma((steps, az_count)),
            dma((steps, az_count)),
            dma((2,)),
            dma((2,)),
        ],
        compiler_params=pltpu.CompilerParams(
            collective_id=0, has_side_effects=True, vmem_limit_bytes=62 * 1024 * 1024
        ),
    )(raw_re, raw_im, ref_blocks[0].T, owners, jnp.asarray(matrices), jnp.asarray(twiddle))
    vmem = pl.BlockSpec(memory_space=pltpu.VMEM)
    return pl.pallas_call(
        functools.partial(stolt_kernel, piece),
        out_shape=[jax.ShapeDtypeStruct(raw_re.shape, jnp.float32)] * 2,
        in_specs=[hbm, smem, vmem],
        out_specs=[hbm, hbm],
        scratch_shapes=[
            pltpu.VMEM((depth * piece, LANES), jnp.float32),
            pltpu.VMEM((2, rows, samples), jnp.float32),
            dma((4,)),
            dma((2, 2)),
        ],
        compiler_params=pltpu.CompilerParams(vmem_limit_bytes=62 * 1024 * 1024),
    )(band, offsets, taps.T)


def body_for(mesh):
    az_count, rg_count = mesh.shape["az"], mesh.shape["rg"]

    def body(raw_re, raw_im, ref_blocks, owners, offsets, taps):
        rows, samples = raw_re.shape
        fits = (
            samples * az_count == LANES * LANES
            and az_count == 8
            and rows == 4 * az_count
            and rg_count == 2
            and ref_blocks.shape[1] == 64
        )
        if fits:
            return tuple(fused_shards(az_count, raw_re, raw_im, ref_blocks, owners, offsets, taps))
        return shards(raw_re, raw_im, ref_blocks, owners, offsets, taps)

    return body


def solution(mesh):
    return jax.shard_map(
        body_for(mesh),
        mesh=mesh,
        in_specs=(
            P("rg", ("scene", "az")),
            P("rg", ("scene", "az")),
            P(("scene", "az"), None, "rg"),
            P("scene"),
            P("rg"),
            P("rg", None),
        ),
        out_specs=(P("rg", ("scene", "az")), P("rg", ("scene", "az"))),
        check_vma=False,
    )
```

```python
import functools
import math

import jax
import jax.numpy as jnp
import ml_dtypes
import numpy as np
from jax import lax
from jax.experimental import pallas as pl
from jax.experimental.pallas import tpu as pltpu
from jax.sharding import PartitionSpec as P

SPLIT = 4
TAPS = 8
REACH = 8
BLOCK = 16


PRECISE = lax.Precision.HIGHEST
PHASE_GAIN = 50.0


def partner_2(value, axis, stride):
    return lax.ppermute(value, axis, [(i, i ^ 1 << stride) for i in range(lax.axis_size(axis))])


def from_root(block, axis, source):
    block = jnp.where(lax.axis_index(axis) == source, block, jnp.zeros_like(block))
    return lax.psum(block, axis)


def padded_2(value, sides, width):
    for axis, dim in sides:
        size, length = (lax.axis_size(axis), value.shape[dim])
        up = [(i, (i + 1) % size) for i in range(size - 1)]
        down = [(j, i) for i, j in up]
        last = lax.slice_in_dim(value, length - width, length, axis=dim)
        initial = lax.slice_in_dim(value, 0, width, axis=dim)
        before = lax.ppermute(last, axis, up)
        after = lax.ppermute(initial, axis, down)
        value = jnp.concatenate([before, value, after], axis=dim)
    return value


def angles(numerator, denominator, sign_value):
    return sign_value * 2.0 * math.pi * numerator.astype(jnp.float32) / denominator


def rotate(signal, cosine, sine_part):
    real_part = signal[0] * cosine - signal[1] * sine_part
    imag_part = signal[0] * sine_part + signal[1] * cosine
    return jnp.stack([real_part, imag_part])


def dft_table(length_n, sign_value):
    counter = jnp.arange(length_n, dtype=jnp.int32)
    turn_count = counter[:, None] * counter[None, :] % length_n
    angle_set = angles(turn_count, length_n, sign_value)
    return (jnp.cos(angle_set), jnp.sin(angle_set))


def complex_apply(einsum_form, cosine, sine_part, signal):
    real_part = jnp.einsum(einsum_form, cosine, signal[0], precision=PRECISE) - jnp.einsum(
        einsum_form, sine_part, signal[1], precision=PRECISE
    )
    imag_part = jnp.einsum(einsum_form, cosine, signal[1], precision=PRECISE) + jnp.einsum(
        einsum_form, sine_part, signal[0], precision=PRECISE
    )
    return jnp.stack([real_part, imag_part])


def local_dft(signal, sign_value):
    rg_cols = signal.shape[1]
    az_rows = signal.shape[2]
    inner_len = az_rows // SPLIT
    shaped = signal.reshape(2, rg_cols, SPLIT, inner_len)
    first_cos, first_sin = dft_table(SPLIT, sign_value)
    first_pass = complex_apply("aj,cjk->cak", first_cos, first_sin, shaped)
    outer_idx = jnp.arange(SPLIT, dtype=jnp.int32)
    inner_idx = jnp.arange(inner_len, dtype=jnp.int32)
    twist = angles(outer_idx[:, None] * inner_idx[None, :] % az_rows, az_rows, sign_value)
    first_pass = rotate(first_pass, jnp.cos(twist)[None, :, :], jnp.sin(twist)[None, :, :])
    second_cos, second_sin = dft_table(inner_len, sign_value)
    second_pass = complex_apply("bk,cak->cba", second_cos, second_sin, first_pass)
    return second_pass.reshape(2, rg_cols, az_rows)


def butterfly_down(signal, az_place, bit_count):
    for bit_num in reversed(range(bit_count)):
        half_span = 1 << bit_num
        partner = partner_2(signal, "az", bit_num)
        is_upper = az_place >> bit_num & 1 == 1
        angle_set = angles(az_place % half_span, 2 * half_span, -1.0)
        difference = rotate(partner - signal, jnp.cos(angle_set), jnp.sin(angle_set))
        signal = jnp.where(is_upper, difference, signal + partner)
    return signal


def butterfly_up(signal, az_place, bit_count):
    for bit_num in range(bit_count):
        half_span = 1 << bit_num
        partner = partner_2(signal, "az", bit_num)
        is_upper = az_place >> bit_num & 1 == 1
        angle_set = angles(az_place % half_span, 2 * half_span, 1.0)
        cosine = jnp.cos(angle_set)
        sine_part = jnp.sin(angle_set)
        lower_new = (signal + rotate(partner, cosine, sine_part)) * 0.5
        upper_new = (partner - rotate(signal, cosine, sine_part)) * 0.5
        signal = jnp.where(is_upper, upper_new, lower_new)
    return signal


def shards(raw_re, raw_im, ref_blocks, owners, offsets, taps):
    rg_cols = raw_re.shape[0]
    az_rows = raw_re.shape[1]
    az_count = lax.axis_size("az")
    az_place = lax.axis_index("az")
    bit_count = az_count.bit_length() - 1
    az_total = az_rows * az_count
    rg_total = rg_cols * lax.axis_size("rg")
    own_block = ref_blocks[0]
    lower_ref = from_root(own_block, "az", owners[0])
    upper_ref = from_root(own_block, "az", owners[1])
    signal = jnp.stack([raw_re, raw_im])
    signal = butterfly_down(signal, az_place, bit_count)
    column = jnp.zeros((), jnp.int32)
    for bit_num in range(bit_count):
        column = column + ((az_place >> bit_num & 1) << bit_count - 1 - bit_num)
    row_index = jnp.arange(az_rows, dtype=jnp.int32)
    twist = angles(row_index * column % az_total, az_total, -1.0)
    signal = rotate(signal, jnp.cos(twist)[None, :], jnp.sin(twist)[None, :])
    signal = local_dft(signal, -1.0)
    frequency = column + az_count * row_index
    signed = (frequency + az_total // 2) % az_total - az_total // 2
    az_freq = signed.astype(jnp.float32) / az_total
    rg_index = lax.axis_index("rg") * rg_cols + jnp.arange(rg_cols, dtype=jnp.int32)
    rg_freq = (rg_index.astype(jnp.float32) + 0.5) / (2 * rg_total) - 0.25
    model_phase = PHASE_GAIN * jnp.sqrt((1.0 + rg_freq)[:, None] ** 2 - az_freq[None, :] ** 2)
    ref_rows = own_block.shape[0]
    coarse = frequency * ref_rows // az_total
    slot_index = jnp.where(signed >= 0, ref_rows + coarse, coarse)
    one_hot = (jnp.arange(2 * ref_rows, dtype=jnp.int32)[:, None] == slot_index[None, :]).astype(
        jnp.float32
    )
    both_refs = jnp.concatenate([lower_ref, upper_ref], axis=0)
    picked = jnp.dot(both_refs.T, one_hot, precision=PRECISE)
    phase_all = model_phase + picked
    signal = rotate(signal, jnp.cos(phase_all), jnp.sin(phase_all))
    rim_width = REACH + TAPS // 2
    padded = padded_2(signal, (("rg", 1),), rim_width)
    offset_cols = jnp.repeat(offsets, BLOCK)
    local_cols = jnp.arange(rg_cols, dtype=jnp.int32)
    tap_index = jnp.arange(TAPS, dtype=jnp.int32)
    target = local_cols[:, None] + rim_width + offset_cols[:, None] + tap_index[None, :] - TAPS // 2
    padded_index = jnp.arange(rg_cols + 2 * rim_width, dtype=jnp.int32)
    hits = (padded_index[:, None, None] == target[None, :, :]).astype(jnp.float32)
    band_matrix = jnp.sum(hits * taps[None, :, :], axis=2)
    signal = jnp.einsum("zma,mi->zia", padded, band_matrix, precision=PRECISE)
    signal = local_dft(signal, 1.0) / az_rows
    twist_back = angles(row_index * column % az_total, az_total, 1.0)
    signal = rotate(signal, jnp.cos(twist_back)[None, :], jnp.sin(twist_back)[None, :])
    signal = butterfly_up(signal, az_place, bit_count)
    return (signal[0], signal[1])


LANES = 128
MESH = pl.DeviceIdType.MESH
RIM = REACH + TAPS // 2
TWO_PI_HI = 6.28125
TWO_PI_LO = 2.0 * math.pi - TWO_PI_HI


def split_np(matrix):
    high = matrix.astype(np.float32).astype(ml_dtypes.bfloat16)
    low = (matrix - high.astype(np.float64)).astype(np.float32).astype(ml_dtypes.bfloat16)
    return np.stack([high, low])


def tables(az_count):
    inner = LANES // az_count
    grid = np.arange(LANES)
    angle = 2.0 * np.pi * (np.outer(grid, grid) % LANES) / LANES
    cos, sin = np.cos(angle), -np.sin(angle)
    forward = [[cos, -sin], [sin, cos]]
    inverse = [[cos, sin], [-sin, cos]]
    order = np.arange(2 * LANES).reshape(2, az_count, inner).transpose(1, 0, 2).reshape(-1)
    left_in = np.block(forward)[:, order]
    right_in = np.block([[forward[o][c].T for o in range(2)] for c in range(2)])
    right_out = np.block([[inverse[o][c].T for o in range(2)] for c in range(2)])
    left_out = np.block(inverse)[order, :] / (LANES * LANES)
    matrices = np.stack([split_np(m) for m in (left_in, right_in, right_out, left_out)])
    turn = 2.0 * np.pi * np.outer(grid, grid) / (LANES * LANES)
    twiddle = np.stack([np.cos(turn), -np.sin(turn)]).astype(np.float32)
    return matrices, twiddle


def split(value):
    high = value.astype(jnp.bfloat16)
    low = (value - high.astype(jnp.float32)).astype(jnp.bfloat16)
    return high, low


def dot(a, b):
    return jnp.dot(a, b, preferred_element_type=jnp.float32)


def left_apply(table, value):
    high, low = split(value)
    return dot(table[0], high) + (dot(table[0], low) + dot(table[1], high))


def right_apply(value, table):
    high, low = split(value)
    return dot(high, table[0]) + (dot(low, table[0]) + dot(high, table[1]))


def cos_sin(phase):
    turns = jnp.floor(phase * (0.5 / math.pi) + 0.5)
    rest = (phase - turns * TWO_PI_HI) - turns * TWO_PI_LO
    half = rest * 0.5
    square = half * half
    sine = jnp.full_like(square, -1.0 / math.factorial(11))
    for power in (9, 7, 5, 3, 1):
        sine = sine * square + (-1.0) ** (power // 2) / math.factorial(power)
    sine = sine * half
    cosine = jnp.full_like(square, 1.0 / math.factorial(12))
    for power in (10, 8, 6, 4, 2, 0):
        cosine = cosine * square + (-1.0) ** (power // 2) / math.factorial(power)
    return 1.0 - 2.0 * sine * sine, 2.0 * sine * cosine


def focus_kernel(
    az_count,
    depth,
    re_hbm,
    im_hbm,
    refs_hbm,
    owners,
    matrices_hbm,
    twiddle_hbm,
    band,
    raw,
    refs,
    matrices,
    twiddle,
    outgoing,
    incoming,
    ref_out,
    ref_in,
    filt,
    focused,
    blank,
    chosen,
    raw_sem,
    const_sem,
    own_sem,
    ref_send,
    ref_recv,
    in_send,
    in_recv,
    back_send,
    back_recv,
    rim_send,
    rim_recv,
):
    rows = re_hbm.shape[0]
    inner = re_hbm.shape[1] // LANES
    piece = 2 * inner
    steps = rows // az_count
    me = lax.axis_index("az")
    core = lax.axis_index("rg")
    peers = []
    for flips in sorted(range(1, az_count), reverse=True):
        peer = me
        for bit in (1 << b for b in range(az_count.bit_length())):
            if flips & bit:
                peer = peer + bit - 2 * bit * lax.rem(lax.div(peer, bit), 2)
        peers.append(peer)
    sources = peers
    sibling = 1 - core
    def group_of(step):
        return step + (1 - core) * (steps - 1 - 2 * step)

    def each(count, action):
        def run(index, carry):
            action(index)
            return carry

        lax.fori_loop(0, count, run, 0)

    def raw_copy(step, comp):
        group = pl.ds(pl.multiple_of(group_of(step) * az_count, az_count), az_count)
        hbm = (re_hbm, im_hbm)[comp]
        return pltpu.make_async_copy(hbm.at[group, :], raw.at[comp, step], raw_sem.at[step, comp])

    load_refs = pltpu.make_async_copy(refs_hbm, refs, const_sem.at[2])
    load_refs.start()
    for step in range(steps):
        for comp in range(2):
            raw_copy(step, comp).start()

    barrier = pltpu.get_barrier_semaphore()
    for peer in peers:
        pl.semaphore_signal(barrier, inc=1, device_id={"az": peer}, device_id_type=MESH)
    pl.semaphore_signal(barrier, inc=1, device_id={"rg": sibling}, device_id_type=MESH)
    load_matrices = pltpu.make_async_copy(matrices_hbm, matrices, const_sem.at[0])
    load_twiddle = pltpu.make_async_copy(twiddle_hbm, twiddle, const_sem.at[1])
    load_matrices.start()
    load_twiddle.start()

    def at(start, count):
        return pl.ds(start * piece if isinstance(start, int) else pl.multiple_of(start * piece, piece), count * piece)

    ref_rows = refs.shape[1]
    coarse = lax.broadcasted_iota(jnp.int32, (ref_rows, LANES), 0)
    column = lax.broadcasted_iota(jnp.int32, (ref_rows, LANES), 1)
    spread = (coarse == column // (LANES // ref_rows)).astype(jnp.float32)
    load_refs.wait()
    wide = jnp.dot(refs[...], spread, precision=PRECISE, preferred_element_type=jnp.float32)
    ref_out[...] = jnp.zeros_like(ref_out)
    for dest in range(az_count):
        for group in range(steps):
            row = group * az_count + dest
            ref_out[dest, group : group + 1, :] = wide[row : row + 1, :]

    def ref_copy(s, peer, source):
        return pltpu.make_async_remote_copy(
            src_ref=ref_out.at[peer],
            dst_ref=ref_in.at[source],
            send_sem=ref_send.at[s],
            recv_sem=ref_recv.at[source],
            device_id={"az": peer},
            device_id_type=MESH,
        )

    def in_copy(step, s, peer, source):
        return pltpu.make_async_remote_copy(
            src_ref=outgoing.at[at(group_of(step) * az_count + peer, 1), :],
            dst_ref=incoming.at[at(group_of(step) * az_count + source, 1), :],
            send_sem=in_send.at[step, s],
            recv_sem=in_recv.at[step, source],
            device_id={"az": peer},
            device_id_type=MESH,
        )

    def back_copy(step, s, peer, source):
        return pltpu.make_async_remote_copy(
            src_ref=focused.at[at(group_of(step) * az_count + peer, 1), :],
            dst_ref=band.at[at(RIM + group_of(step) * az_count + source, 1), :],
            send_sem=back_send.at[step, s],
            recv_sem=back_recv.at[step, source],
            device_id={"az": peer},
            device_id_type=MESH,
        )

    def own_copy(step):
        row = group_of(step) * az_count + me
        return pltpu.make_async_copy(focused.at[at(row, 1), :], band.at[at(RIM + row, 1), :], own_sem.at[step])

    def rim_copy(step):
        count = (az_count, RIM - az_count)[step]
        first = ((rows - az_count, rows - RIM)[step], (0, az_count)[step])
        place = ((RIM - az_count, 0)[step], (RIM + rows, RIM + rows + az_count)[step])
        return pltpu.make_async_remote_copy(
            src_ref=band.at[at(RIM + first[0] * (1 - core) + first[1] * core, count), :],
            dst_ref=band.at[at(place[0] * (1 - core) + place[1] * core, count), :],
            send_sem=rim_send.at[step],
            recv_sem=rim_recv.at[step],
            device_id={"rg": sibling},
            device_id_type=MESH,
        )

    def rim_arrival(step):
        count = (az_count, RIM - az_count)[step]
        place = ((RIM - az_count, 0)[step], (RIM + rows, RIM + rows + az_count)[step])
        return pltpu.make_async_remote_copy(
            src_ref=band.at[at(RIM, count), :],
            dst_ref=band.at[at(place[0] * core + place[1] * (1 - core), count), :],
            send_sem=rim_send.at[step],
            recv_sem=rim_recv.at[step],
            device_id={"rg": sibling},
            device_id_type=MESH,
        )

    def prepare(step):
        for comp in range(2):
            raw_copy(step, comp).wait()
            for i in range(inner):
                place = group_of(step) * (az_count * piece) + (comp * inner + i)
                outgoing[pl.ds(place, az_count, stride=piece), :] = raw[comp, step, :, i * LANES : (i + 1) * LANES]

    def send(step):
        for s, peer in enumerate(peers):
            in_copy(step, s, peer, me).start()
        own = at(group_of(step) * az_count + me, 1)
        incoming[own, :] = outgoing[own, :]

    each(steps, prepare)
    pl.semaphore_wait(barrier, az_count)
    for s, peer in enumerate(peers):
        ref_copy(s, peer, me).start()
    each(steps, send)

    ref_in[me] = ref_out[me]
    blank[...] = jnp.zeros_like(blank)
    spare = depth - rows - 2 * RIM
    clear_rim = pltpu.make_async_copy(blank, band.at[at((RIM + rows) * core, RIM), :], const_sem.at[3])
    clear_rim.start()
    clear_spare = pltpu.make_async_copy(
        blank.at[at(0, spare), :], band.at[at(depth - spare, spare), :], const_sem.at[4]
    )
    clear_spare.start()

    for s, source in enumerate(sources):
        ref_copy(s, peers[s], source).wait_recv()
    lane = lax.broadcasted_iota(jnp.int32, ref_in.shape[1:], 1)
    picked = jnp.zeros(ref_in.shape[1:], jnp.float32)
    for source in range(az_count):
        wanted = jnp.where(lane < LANES // 2, owners[1], owners[0]) == source
        picked = jnp.where(wanted, ref_in[source], picked)
    chosen[...] = picked
    az_total = LANES * LANES
    low = lax.broadcasted_iota(jnp.int32, (LANES, LANES), 0)
    high = lax.broadcasted_iota(jnp.int32, (LANES, LANES), 1)
    frequency = low + LANES * high
    signed = jnp.where(frequency >= az_total // 2, frequency - az_total, frequency)
    az_freq = signed.astype(jnp.float32) / az_total
    az_square = az_freq * az_freq
    def make_filter(group):
        index = core * rows + group * az_count + me
        rg_freq = 1.0 + ((index.astype(jnp.float32) + 0.5) * (1.0 / (4 * rows)) - 0.25)
        phase = PHASE_GAIN * jnp.sqrt(rg_freq * rg_freq - az_square) + chosen[pl.ds(group, 1), :]
        cosine, sine = cos_sin(phase)
        filt[group, 0] = cosine
        filt[group, 1] = sine

    each(steps, make_filter)

    load_matrices.wait()
    load_twiddle.wait()
    def arrive(step):
        own_copy(step).wait()
        for s, source in enumerate(sources):
            back_copy(step, s, peers[s], source).wait_recv()

    def focus(step):
        group = group_of(step)
        for s, source in enumerate(sources):
            in_copy(step, s, peers[s], source).wait_recv()
        whole = at(group * az_count, az_count)
        value = left_apply((matrices[0, 0], matrices[0, 1]), incoming[whole, :])
        cosine, sine = twiddle[0], twiddle[1]
        real, imag = value[:LANES], value[LANES:]
        value = jnp.concatenate([real * cosine - imag * sine, real * sine + imag * cosine], axis=1)
        value = right_apply(value, (matrices[1, 0], matrices[1, 1]))
        real, imag = value[:, :LANES], value[:, LANES:]
        cosine, sine = filt[group, 0], filt[group, 1]
        value = jnp.concatenate([real * cosine - imag * sine, real * sine + imag * cosine], axis=1)
        value = right_apply(value, (matrices[2, 0], matrices[2, 1]))
        real, imag = value[:, :LANES], value[:, LANES:]
        cosine, sine = twiddle[0], twiddle[1]
        value = jnp.concatenate([real * cosine + imag * sine, imag * cosine - real * sine], axis=0)
        focused[whole, :] = left_apply((matrices[3, 0], matrices[3, 1]), value)
        for s, peer in enumerate(peers):
            back_copy(step, s, peer, me).start()
        own_copy(step).start()

    each(steps, focus)
    for step in range(2):
        arrive(step)
        rim_copy(step).start()
    clear_rim.wait()
    clear_spare.wait()
    each(steps - 2, lambda step: arrive(step + 2))
    for step in range(2):
        rim_arrival(step).wait_recv()

    def sent(step):
        for s, peer in enumerate(peers):
            in_copy(step, s, peer, me).wait_send()
            back_copy(step, s, peer, me).wait_send()

    each(steps, sent)
    for s, peer in enumerate(peers):
        ref_copy(s, peer, me).wait_send()
    for step in range(2):
        rim_copy(step).wait_send()


def stolt_kernel(piece, band_hbm, offsets, taps, out_re, out_im, band, image, in_sem, out_sem):
    depth = band.shape[0] // piece
    inner = piece // 2
    half = inner // 2
    rows = out_re.shape[0]
    outs = (out_re, out_im)
    loads = in_sem.shape[0]

    def load(part):
        lines = pl.ds(part * (band.shape[0] // loads), band.shape[0] // loads)
        return pltpu.make_async_copy(band_hbm.at[lines, :], band.at[lines, :], in_sem.at[part])

    def save(comp, part):
        columns = pl.ds(part * half * LANES, half * LANES)
        return pltpu.make_async_copy(image.at[comp, :, columns], outs[comp].at[:, columns], out_sem.at[comp, part])

    for part in range(loads):
        load(part).start()
    slot = lax.broadcasted_iota(jnp.int32, (depth, rows), 0)
    target = lax.broadcasted_iota(jnp.int32, (depth, rows), 1)
    target_block = target // BLOCK
    for block in range(rows // BLOCK):
        target = jnp.where(target_block == block, target + offsets[block], target)
    weights = jnp.zeros((depth, rows), jnp.float32)
    for tap in range(TAPS):
        weights = weights + jnp.where(slot == target + (RIM + tap - TAPS // 2), taps[tap : tap + 1, :], 0.0)
    high, low = split(weights.T)
    weights = jnp.concatenate([high, high, low], axis=1)
    for part in range(loads):
        load(part).wait()
    for comp in range(2):
        for part in range(2):
            for i in range(part * half, part * half + half, 2):
                value = jnp.concatenate(
                    [band[pl.ds(comp * inner + i + j, depth, stride=piece), :] for j in range(2)], axis=1
                )
                high, low = split(value)
                value = dot(weights, jnp.concatenate([high, low, high], axis=0))
                image[comp, :, i * LANES : (i + 2) * LANES] = value
            save(comp, part).start()
    for comp in range(2):
        for part in range(2):
            save(comp, part).wait()


def fused_shards(az_count, raw_re, raw_im, ref_blocks, owners, offsets, taps):
    rows, samples = raw_re.shape
    ref_rows = ref_blocks.shape[1]
    piece = 2 * samples // LANES
    steps = rows // az_count
    depth = -(-(rows + 2 * RIM) // 16) * 16
    matrices, twiddle = tables(az_count)
    smem = pl.BlockSpec(memory_space=pltpu.SMEM)
    hbm = pl.BlockSpec(memory_space=pl.ANY)
    dma = pltpu.SemaphoreType.DMA
    flat = pltpu.VMEM((rows * piece, LANES), jnp.float32)
    band = pl.pallas_call(
        functools.partial(focus_kernel, az_count, depth),
        out_shape=jax.ShapeDtypeStruct((depth * piece, LANES), jnp.float32),
        in_specs=[hbm, hbm, hbm, smem, hbm, hbm],
        out_specs=hbm,
        scratch_shapes=[
            pltpu.VMEM((2, steps, az_count, samples), jnp.float32),
            pltpu.VMEM((rows, ref_rows), jnp.float32),
            pltpu.VMEM(matrices.shape, jnp.bfloat16),
            pltpu.VMEM(twiddle.shape, jnp.float32),
            flat,
            flat,
            pltpu.VMEM((az_count, 8, LANES), jnp.float32),
            pltpu.VMEM((az_count, 8, LANES), jnp.float32),
            pltpu.VMEM((steps, 2, LANES, LANES), jnp.float32),
            flat,
            pltpu.VMEM((RIM * piece, LANES), jnp.float32),
            pltpu.VMEM((8, LANES), jnp.float32),
            dma((steps, 2)),
            dma((5,)),
            dma((steps,)),
            dma((az_count,)),
            dma((az_count,)),
            dma((steps, az_count)),
            dma((steps, az_count)),
            dma((steps, az_count)),
            dma((steps, az_count)),
            dma((2,)),
            dma((2,)),
        ],
        compiler_params=pltpu.CompilerParams(
            collective_id=0, has_side_effects=True, vmem_limit_bytes=62 * 1024 * 1024
        ),
    )(raw_re, raw_im, ref_blocks[0].T, owners, jnp.asarray(matrices), jnp.asarray(twiddle))
    vmem = pl.BlockSpec(memory_space=pltpu.VMEM)
    return pl.pallas_call(
        functools.partial(stolt_kernel, piece),
        out_shape=[jax.ShapeDtypeStruct(raw_re.shape, jnp.float32)] * 2,
        in_specs=[hbm, smem, vmem],
        out_specs=[hbm, hbm],
        scratch_shapes=[
            pltpu.VMEM((depth * piece, LANES), jnp.float32),
            pltpu.VMEM((2, rows, samples), jnp.float32),
            dma((4,)),
            dma((2, 2)),
        ],
        compiler_params=pltpu.CompilerParams(vmem_limit_bytes=62 * 1024 * 1024),
    )(band, offsets, taps.T)


def body_for(mesh):
    az_count, rg_count = mesh.shape["az"], mesh.shape["rg"]

    def body(raw_re, raw_im, ref_blocks, owners, offsets, taps):
        rows, samples = raw_re.shape
        fits = (
            samples * az_count == LANES * LANES
            and az_count == 8
            and rows == 4 * az_count
            and rg_count == 2
            and ref_blocks.shape[1] == 64
        )
        if fits:
            return tuple(fused_shards(az_count, raw_re, raw_im, ref_blocks, owners, offsets, taps))
        return shards(raw_re, raw_im, ref_blocks, owners, offsets, taps)

    return body


def solution(mesh):
    return jax.shard_map(
        body_for(mesh),
        mesh=mesh,
        in_specs=(
            P("rg", ("scene", "az")),
            P("rg", ("scene", "az")),
            P(("scene", "az"), None, "rg"),
            P("scene"),
            P("rg"),
            P("rg", None),
        ),
        out_specs=(P("rg", ("scene", "az")), P("rg", ("scene", "az"))),
        check_vma=False,
    )
```
